256 devices in a mesh: ep: 64 (over z, y, core), kv: 4 (over x).
Axes of the slice: x: 4, y: 4, z: 8, core: 2. Of those that a mesh axis runs over, the one named last changes fastest.
Arguments:
- queries: bfloat16 [128, 2048], P('ep'), may hold values from -10 to 10
- key_pool: bfloat16 [1536, 128, 2048], P(('ep', 'kv')), may hold values from -4 to 4
- value_pool: bfloat16 [1536, 128, 2048], P(('ep', 'kv')), may hold values from -15 to 15
- page_table: int32 [128, 4, 3], P('ep', 'kv'), may hold values from 0 to 5, as said below
- lengths: int32 [128], P('ep'), may hold values from 2 to 1536, as said below
- prefill_attn: bfloat16 [8064, 2048], P('ep'), may hold values from -3 to 3
- residual: bfloat16 [8192, 2048], P('ep', 'kv'), may hold values from -64 to 64
- w_out: bfloat16 [2048, 2048], P(None, 'kv'), may hold values from -0.125 to 0.125
- norm_gain: float32 [2048], P('kv'), may hold values from 0.1 to 1.9
- router: bfloat16 [2048, 64], P('kv'), may hold values from -0.125 to 0.125
- w_gate: bfloat16 [64, 2048, 1024], P('ep', None, 'kv'), may hold values from -0.125 to 0.125
- w_up: bfloat16 [64, 2048, 1024], P('ep', None, 'kv'), may hold values from -0.125 to 0.125
- w_down: bfloat16 [64, 1024, 2048], P('ep', 'kv'), may hold values from -0.375 to 0.375
- final_gain: float32 [2048], P('kv'), may hold values from 0.1 to 1.9
- routes: int32 [8192, 8], P('ep'), may hold values from 0 to 63, all different within a row; in each aligned block of 128 rows (0 to 127, 128 to 255, ...) at most 32 rows name the same one
Outputs:
- output: bfloat16 [8192, 2048], P('ep', 'kv')
The draws below stay inside these ranges and needn't reach their ends.
Inputs may be any that keep to these rules, and one draw needn't show every extreme that they name: `page_table`: the 2 x 3 entries of one group of requests at one holder are a permutation of 0 to 5. `lengths`: some request has length exactly 1536. `routes`: each row names 8 different experts; in the rows of one index of ep (aligned blocks of 128 rows) no expert is named more than 32 times, a bound that some block reaches.
All inputs are finite; a program needn't handle non-finite values.
Results may differ from the reference program's by a relative error of at most 0.009.
Values may be sent and summed in bfloat16 or wider, within the bound.
A program may use at most 128 MiB of HBM per device.

```python
import math
import jax
import jax.numpy as jnp
import numpy as np
from jax import lax

D = 2048
HEADS = 16
HEAD_DIM = 128
FF = 1024
TOP = 8
PAGE = 128
DEC_DEV = 2
PPR = 3
PRE_DEV = 126
EXPERTS = 64
ROWS = 128
CAP = 32
POOL = 6
MAXLEN = 1536
REQUESTS = 128
PREFILL = 8064
TOKENS = 8192
PAGES = 1536
N_EP = 64
N_KV = 4


def draw_queries(key, part):
    result = jax.random.truncated_normal(jax.random.fold_in(key, 1), -4.0, 4.0, (REQUESTS, HEADS, HEAD_DIM), jnp.float32)
    return result.reshape(REQUESTS, D).astype(jnp.bfloat16)


def draw_key_pool(key, part):
    result = jax.random.truncated_normal(jax.random.fold_in(key, 3), -4.0, 4.0, (PAGES, PAGE, HEADS, HEAD_DIM), jnp.float32)
    return result.reshape(PAGES, PAGE, D).astype(jnp.bfloat16)


def draw_residual(key, part):
    column_pos = jnp.arange(D, dtype=jnp.float32) / (D - 1)
    spread = jnp.exp(math.log(10.0) * jax.random.uniform(jax.random.fold_in(key, 3), (D,), jnp.float32))
    noise = jax.random.truncated_normal(jax.random.fold_in(key, 4), -4.0, 4.0, (TOKENS, D), jnp.float32)
    rising = 0.1 * jnp.exp(math.log(3.0) * column_pos)
    row_scale = jnp.exp(jax.random.uniform(jax.random.fold_in(key, 5), (TOKENS, 1), jnp.float32, math.log(0.5), math.log(2.0)))
    return (noise * rising[None, :] * spread[None, :] * row_scale).astype(jnp.bfloat16)


def draw_page_table(key, part):
    device_keys = jax.random.split(jax.random.fold_in(key, 7), N_EP * N_KV)
    orders = jax.vmap(lambda device_key: jax.random.permutation(device_key, POOL))(device_keys)
    orders = orders.reshape(N_EP, N_KV, DEC_DEV, PPR).transpose(0, 2, 1, 3)
    return orders.reshape(REQUESTS, N_KV, PPR).astype(jnp.int32)


def draw_lengths(key, part):
    trials = jax.random.randint(jax.random.fold_in(key, 8), (3, REQUESTS), 2, MAXLEN + 1, jnp.int32)
    shortest = jnp.min(trials, axis=0)
    longest_at = jax.random.randint(jax.random.fold_in(key, 9), (), 0, REQUESTS, jnp.int32)
    return shortest.at[longest_at].set(MAXLEN).astype(jnp.int32)


def levels(rng, shape, shards, least, high):
    factor_of = 1.0
    for dim, shards_of in shards:
        heights = jax.random.uniform(jax.random.fold_in(jax.random.fold_in(rng, 6), dim), (shards_of,), jnp.float32, least / len(shards), high / len(shards))
        factor_of = factor_of * jnp.repeat(jnp.exp(heights), shape[dim] // shards_of).reshape((-1,) + (1,) * (len(shape) - 1 - dim))
    return factor_of


def assign_block(own_key, own, number, rows, count, top, most, skew):
    order = jax.random.permutation(own_key, count)
    heavy_load, common = portions_of(count, rows * top, most, skew, True), portions_of(count, rows * top, most, skew, False)
    places = jnp.arange(count)

    def named(tallies, rotation):
        used = int((tallies > 0).sum())
        fixed = max(1, used // 4)
        passed = fixed + (places - fixed + rotation * (used - fixed)) % max(1, count - fixed)
        return jnp.zeros((count,), jnp.int32).at[order[jnp.where(places < fixed, places, passed)]].set(jnp.asarray(tallies, jnp.int32))

    tallies = jnp.where(number % 4 == 0, named(heavy_load, number // 4), named(common, number - number // 4 - 1))
    mixed = jax.random.permutation(jax.random.fold_in(own, 3), count)
    source_of, sink = mixed[0:count // 2 * 2:2], mixed[1:count // 2 * 2:2]
    slack = jnp.minimum(tallies[source_of] - 1, most - tallies[sink]) // 2
    slack = jnp.where((source_of == order[0]) | (sink == order[0]) | (tallies[sink] == 0), 0, jnp.maximum(slack, 0))
    passed = jax.random.randint(jax.random.fold_in(own, 4), (count // 2,), 0, 1 << 20) % (slack + 1)
    tallies = tallies.at[source_of].add(-passed).at[sink].add(passed)
    labels = jnp.searchsorted(jnp.cumsum(tallies), jnp.arange(rows * top), side="right").astype(jnp.int32)
    grid = labels.reshape(top, rows).T
    grid = grid[jax.random.permutation(jax.random.fold_in(own, 1), rows)]
    rotation = jax.random.randint(jax.random.fold_in(own, 2), (rows, 1), 0, top)
    return jnp.take_along_axis(grid, (jnp.arange(top)[None, :] + rotation) % top, axis=1)


def portions_of(count, total, limit, lean, full):
    loads = [(1 << 20) // math.isqrt(grade ** lean) + 1 for grade in range(1, count + 1)]
    largest = limit if full else min(limit, max(-(-total // count), total * loads[0] // sum(loads)))
    least = 1 if total - largest >= count - 1 else 0
    holding, surplus = [largest] + [least] * (count - 1), total - largest - least * (count - 1)
    while surplus > 0:
        candidates = [i for i in range(1, count) if holding[i] < largest] or [i for i in range(1, count) if holding[i] < limit]
        mass, budget = sum([loads[i] for i in candidates]), surplus
        for i in candidates:
            addition = min(limit - holding[i], max(1, budget * loads[i] // mass), surplus)
            holding[i] = holding[i] + addition
            surplus = surplus - addition
    return np.array(holding)


def gaussian(rng, dims, width, limit, shards=(), kind=jnp.bfloat16):
    entries = width * jax.random.normal(rng, dims, jnp.float32)
    if shards:
        entries = entries * levels(rng, dims, shards, -0.22, 0.18)
    return jnp.clip(entries, -limit, limit).astype(kind)


def setup_inputs(seed: int = 0) -> dict:
    key_of = jax.random.split(jax.random.key(seed), 16)
    queries = draw_queries(jax.random.fold_in(key_of[15], 71), 0)
    key_pool = draw_key_pool(jax.random.fold_in(key_of[15], 71), 0)
    value_pool = gaussian(key_of[2], (PAGES, PAGE, D), 3.0, 15.0, ((0, 256),))
    page_table = draw_page_table(jax.random.fold_in(key_of[15], 71), 0)
    lengths = draw_lengths(jax.random.fold_in(key_of[15], 71), 0)
    prefill_attn = gaussian(key_of[5], (PREFILL, D), 0.5, 3.0, ((0, 64),))
    residual = draw_residual(jax.random.fold_in(key_of[15], 71), 0)
    w_out = gaussian(key_of[7], (D, D), D ** -0.5, 0.125, ((1, 4),))
    norm_gain = jnp.clip(1.0 + 0.18 * jax.random.normal(key_of[8], (D,), jnp.float32), 0.1, 1.9)
    router = gaussian(key_of[9], (D, EXPERTS), D ** -0.5, 0.125, ((0, 4),))
    w_gate = gaussian(key_of[10], (EXPERTS, D, FF), D ** -0.5, 0.125, ((0, 64), (2, 4)))
    w_up = gaussian(key_of[11], (EXPERTS, D, FF), D ** -0.5, 0.125, ((0, 64), (2, 4)))
    w_down = gaussian(key_of[12], (EXPERTS, FF, D), (FF // 4) ** -0.5, 0.375, ((0, 64), (1, 4)))
    final_gain = jnp.clip(1.0 + 0.18 * jax.random.normal(key_of[13], (D,), jnp.float32), 0.1, 1.9)
    routes_keys = jax.random.split(jax.random.fold_in(key_of[14], 1), TOKENS // ROWS)
    routes_turns = jax.random.permutation(jax.random.fold_in(key_of[14], 3), TOKENS // ROWS)
    routes = jax.vmap(lambda own, number: assign_block(jax.random.fold_in(key_of[14], 2), own, number, ROWS, EXPERTS, TOP, CAP, 2))(routes_keys, routes_turns).reshape((TOKENS, TOP))
    return dict(queries=queries, key_pool=key_pool, value_pool=value_pool, page_table=page_table, lengths=lengths, prefill_attn=prefill_attn, residual=residual, w_out=w_out, norm_gain=norm_gain, router=router, w_gate=w_gate, w_up=w_up, w_down=w_down, final_gain=final_gain, routes=routes)


epsilon = 1e-06

def decode_attention(queries, key_pool, value_pool, page_table, lengths):
    total_pages = PPR * N_KV
    page_ids = jnp.arange(total_pages, dtype=jnp.int32)
    holder_of = page_ids % N_KV
    column = page_ids // N_KV

    def one_request(request):
        group_index = request // DEC_DEV
        local_page = page_table[request][holder_of, column]
        pool_index = (group_index * N_KV + holder_of) * POOL + local_page
        key_rows = key_pool[pool_index].reshape(total_pages * PAGE, HEADS, HEAD_DIM).astype(jnp.float32)
        value_rows = value_pool[pool_index].reshape(total_pages * PAGE, HEADS, HEAD_DIM).astype(jnp.float32)
        query_heads = queries[request].reshape(HEADS, HEAD_DIM).astype(jnp.float32)
        scores = jnp.einsum('hd,thd->ht', query_heads, key_rows, precision=lax.Precision.HIGHEST) / math.sqrt(HEAD_DIM)
        visible = jnp.arange(total_pages * PAGE, dtype=jnp.int32) < lengths[request]
        masked = jnp.where(visible[None, :], scores, -jnp.inf)
        top_score = lax.optimization_barrier(jnp.max(masked, axis=1, keepdims=True))
        weights = jnp.where(visible[None, :], jnp.exp(masked - top_score), 0.0)
        weights = weights / lax.optimization_barrier(jnp.sum(weights, axis=1, keepdims=True))
        result = jnp.einsum('ht,thd->hd', weights, value_rows, precision=lax.Precision.HIGHEST)
        return result.reshape(D).astype(jnp.bfloat16)
    return lax.map(one_request, jnp.arange(REQUESTS, dtype=jnp.int32))

def reference(queries, key_pool, value_pool, page_table, lengths, prefill_attn, residual, w_out, norm_gain, router, w_gate, w_up, w_down, final_gain, routes):
    decode_attn = decode_attention(queries, key_pool, value_pool, page_table, lengths)
    attn_rows = jnp.concatenate([prefill_attn.reshape(N_EP, PRE_DEV, D), decode_attn.reshape(N_EP, DEC_DEV, D)], axis=1).reshape(TOKENS, D)
    hidden_state = residual.astype(jnp.float32) + jnp.dot(attn_rows, w_out, preferred_element_type=jnp.float32)
    inv_first = lax.rsqrt(lax.optimization_barrier(jnp.mean(hidden_state * hidden_state, axis=1)) + epsilon)
    scaled = (hidden_state * norm_gain).astype(jnp.bfloat16)
    logits = jnp.dot(scaled, router, preferred_element_type=jnp.float32) * inv_first[:, None]
    normed = (hidden_state * norm_gain * inv_first[:, None]).astype(jnp.bfloat16)
    chosen = jnp.take_along_axis(logits, routes, axis=1)
    raised = jnp.exp(chosen)
    gate_weights = raised / lax.optimization_barrier(jnp.sum(raised, axis=1, keepdims=True))
    pair_count = ROWS * TOP
    grouped = routes.reshape(N_EP, pair_count)
    one_hot = (grouped[:, :, None] == jnp.arange(EXPERTS, dtype=jnp.int32)[None, None, :]).astype(jnp.int32)
    earlier = jnp.cumsum(one_hot, axis=1) - one_hot
    slot_index = lax.optimization_barrier(jnp.sum(earlier * one_hot, axis=2))
    group_ids = jnp.arange(N_EP, dtype=jnp.int32)[:, None]
    position = group_ids * CAP + slot_index
    row_ids = group_ids * ROWS + jnp.arange(pair_count, dtype=jnp.int32)[None, :] // TOP
    sources = jnp.zeros((EXPERTS, N_EP * CAP), jnp.int32).at[grouped, position].set(row_ids)
    shares = jnp.zeros((EXPERTS, N_EP * CAP), jnp.float32).at[grouped, position].set(gate_weights.reshape(N_EP, pair_count))
    group_width = FF // N_KV

    def expert_step(running, inputs):
        gate_e, up_e, down_e, rows_from, share_e = inputs
        rows_in = normed[rows_from]
        gate_proj = jnp.dot(rows_in, gate_e, preferred_element_type=jnp.float32)
        up_proj = jnp.dot(rows_in, up_e, preferred_element_type=jnp.float32)
        activation = (jax.nn.silu(gate_proj) * up_proj).astype(jnp.bfloat16)
        summed = jnp.zeros((N_EP * CAP, D), jnp.float32)
        for kv_block in range(N_KV):
            partial_value = jnp.dot(activation[:, kv_block * group_width:(kv_block + 1) * group_width], down_e[kv_block * group_width:(kv_block + 1) * group_width], preferred_element_type=jnp.float32)
            rounded = lax.optimization_barrier(partial_value.astype(jnp.bfloat16))
            summed = summed + rounded.astype(jnp.float32)
        expert_out = summed.astype(jnp.bfloat16)
        return (running.at[rows_from].add(share_e[:, None] * expert_out.astype(jnp.float32)), None)
    mixture, _ = lax.scan(expert_step, jnp.zeros((TOKENS, D), jnp.float32), (w_gate, w_up, w_down, sources, shares))
    combined = hidden_state + mixture
    inv_second = lax.rsqrt(lax.optimization_barrier(jnp.mean(combined * combined, axis=1)) + epsilon)
    return (combined * inv_second[:, None] * final_gain).astype(jnp.bfloat16)
```

```python
import math

import jax
import jax.numpy as jnp
from jax import lax
from jax.sharding import PartitionSpec as P

D = 2048
HEADS = 16
HEAD_DIM = 128
TOP = 8


epsilon = 1e-06
floor_score = -1e30


def split_two(v):
    high = v.astype(jnp.bfloat16)
    low = (v - high.astype(jnp.float32)).astype(jnp.bfloat16)
    return high, low


def per_device(
    queries,
    key_pool,
    value_pool,
    page_table,
    lengths,
    prefill_attn,
    residual,
    w_out,
    norm_gain,
    router,
    w_gate,
    w_up,
    w_down,
    final_gain,
    routes,
):
    holders = lax.axis_size("kv")
    holder = lax.axis_index("kv")
    request_count = queries.shape[0]
    pool_pages, page_rows = key_pool.shape[0], key_pool.shape[1]
    pages_each = page_table.shape[2]
    row_count = residual.shape[0]
    feature_cols = residual.shape[1]
    expert_count = router.shape[1]
    share = min(row_count, 2 * row_count * TOP // expert_count) // holders

    gate_all = lax.all_gather(w_gate[0], "kv", axis=0)
    up_all = lax.all_gather(w_up[0], "kv", axis=0)
    down_all = lax.all_gather(w_down[0], "kv", axis=0)

    tokens = pool_pages * page_rows
    keys = key_pool.reshape(tokens, D)
    values = value_pool.reshape(tokens, D)
    head_of = jnp.arange(D, dtype=jnp.int32) // HEAD_DIM
    on_head = (head_of[None, :] == jnp.arange(HEADS, dtype=jnp.int32)[:, None])
    spread = jnp.where(on_head[None], queries[:, None, :], 0).reshape(request_count * HEADS, D)
    scores = lax.dot_general(
        spread, keys, (((1,), (1,)), ((), ())), preferred_element_type=jnp.float32
    ).reshape(request_count, HEADS, pool_pages, page_rows) / math.sqrt(HEAD_DIM)
    slots = page_table[:, 0, :]
    is_page = slots[:, :, None] == jnp.arange(pool_pages, dtype=jnp.int32)[None, None, :]
    page_number = jnp.arange(pages_each, dtype=jnp.int32) * holders + holder
    start = jnp.sum(jnp.where(is_page, page_number[None, :, None] * page_rows, 0), axis=1)
    owned = jnp.any(is_page, axis=1)
    position = start[:, :, None] + jnp.arange(page_rows, dtype=jnp.int32)[None, None, :]
    visible = (owned[:, :, None] & (position < lengths[:, None, None]))[:, None]
    masked = jnp.where(visible, scores, floor_score)
    local_peak = jnp.max(masked, axis=(2, 3))
    weights = jnp.where(visible, jnp.exp(masked - local_peak[:, :, None, None]), 0.0)
    local_mass = jnp.sum(weights, axis=(2, 3))
    high, low = split_two(weights.reshape(request_count * HEADS, tokens))
    wide = jnp.dot(
        jnp.concatenate([high, low], axis=0), values, preferred_element_type=jnp.float32
    ).reshape(2, request_count, HEADS, D)
    local_sum = jnp.sum(jnp.where(on_head[None], wide[0] + wide[1], 0.0), axis=1)
    pack = jnp.concatenate(
        [local_sum, jnp.repeat(local_peak, HEAD_DIM, axis=1), jnp.repeat(local_mass, HEAD_DIM, axis=1)],
        axis=0,
    )
    packs = lax.all_gather(pack, "kv", axis=0).reshape(holders, 3, request_count, D)
    peaks, masses = packs[:, 1], packs[:, 2]
    factors = jnp.exp(peaks - jnp.max(peaks, axis=0)[None])
    decode_attn = (
        jnp.sum(packs[:, 0] * factors, axis=0) / jnp.sum(masses * factors, axis=0)
    ).astype(jnp.bfloat16)
    attn_rows = jnp.concatenate([prefill_attn, decode_attn], axis=0)
    hidden_state = residual.astype(jnp.float32) + jnp.dot(
        attn_rows, w_out, preferred_element_type=jnp.float32
    )
    scaled = (hidden_state * norm_gain).astype(jnp.bfloat16)
    stats = jnp.concatenate(
        [
            jnp.dot(scaled, router, preferred_element_type=jnp.float32),
            jnp.sum(hidden_state * hidden_state, axis=1, keepdims=True),
            jnp.zeros((row_count, 63), jnp.float32),
        ],
        axis=1,
    )
    stats = jnp.sum(lax.all_gather(stats, "kv", axis=0), axis=0)
    inv_first = lax.rsqrt(stats[:, expert_count : expert_count + 1] / D + epsilon)
    logits = stats[:, :expert_count] * inv_first
    normed = (hidden_state * norm_gain * inv_first).astype(jnp.bfloat16)
    full_rows = lax.all_gather(normed, "kv", axis=1, tiled=True)

    experts = jnp.arange(expert_count, dtype=jnp.int32)
    named = jnp.any(routes[:, :, None] == experts[None, None, :], axis=1)
    raised = jnp.where(named, jnp.exp(logits), 0.0)
    gate_weights = raised / jnp.sum(raised, axis=1, keepdims=True)
    before = jnp.tril(jnp.ones((row_count, row_count), jnp.bfloat16), -1)
    rank = jnp.dot(before, named.astype(jnp.bfloat16), preferred_element_type=jnp.float32)
    code = jnp.where(named, rank, -1.0).astype(jnp.int32)
    mine = holder * share + jnp.arange(share, dtype=jnp.int32)
    at_slot = code[:, :, None] == mine[None, None, :]
    pick = at_slot.astype(jnp.bfloat16).reshape(row_count, expert_count * share)
    outbound = lax.dot_general(
        pick, full_rows, (((0,), (0,)), ((), ())), preferred_element_type=jnp.bfloat16
    ).reshape(expert_count, share, D)
    arrived = lax.all_to_all(outbound, "ep", split_axis=0, concat_axis=0, tiled=True)
    inbound = arrived.reshape(-1, D)
    total = jnp.zeros(inbound.shape, jnp.float32)
    for part in range(gate_all.shape[0]):
        gate_proj = jnp.dot(inbound, gate_all[part], preferred_element_type=jnp.float32)
        up_proj = jnp.dot(inbound, up_all[part], preferred_element_type=jnp.float32)
        activation = (jax.nn.silu(gate_proj) * up_proj).astype(jnp.bfloat16)
        total += jnp.dot(activation, down_all[part], preferred_element_type=jnp.float32)
    expert_out = total.astype(jnp.bfloat16).reshape(arrived.shape)
    returned = lax.all_to_all(expert_out, "ep", split_axis=0, concat_axis=0, tiled=True)
    mix = jnp.where(at_slot, gate_weights[:, :, None], 0.0).reshape(row_count, -1)
    high, low = split_two(mix)
    back = returned.reshape(-1, D)
    mixture = jnp.dot(high, back, preferred_element_type=jnp.float32) + jnp.dot(
        low, back, preferred_element_type=jnp.float32
    )
    parts = mixture.astype(jnp.bfloat16).reshape(row_count, holders, feature_cols)
    parts = lax.all_to_all(parts.transpose(1, 0, 2), "kv", split_axis=0, concat_axis=0, tiled=True)
    combined = hidden_state + jnp.sum(parts.astype(jnp.float32), axis=0)
    square_two = lax.psum(jnp.sum(combined * combined, axis=1), "kv")
    return (combined * lax.rsqrt(square_two / D + epsilon)[:, None] * final_gain).astype(
        jnp.bfloat16
    )


def solution(mesh):
    placed = (
        P("ep", None),
        P(("ep", "kv"), None, None),
        P(("ep", "kv"), None, None),
        P("ep", "kv", None),
        P("ep"),
        P("ep", None),
        P("ep", "kv"),
        P(None, "kv"),
        P("kv"),
        P("kv", None),
        P("ep", None, "kv"),
        P("ep", None, "kv"),
        P("ep", "kv", None),
        P("kv"),
        P("ep", None),
    )
    return jax.shard_map(
        per_device, mesh=mesh, in_specs=placed, out_specs=P("ep", "kv"), check_vma=False
    )
```

```python
import math

import jax
import jax.numpy as jnp
from jax import lax
from jax.experimental import pallas as pl
from jax.experimental.pallas import tpu as pltpu
from jax.sharding import PartitionSpec as P

HEAD_DIM = 128
TOP = 8

epsilon = 1e-06
floor_score = -1e30
MESH = pl.DeviceIdType.MESH


def split_two(v):
    high = v.astype(jnp.bfloat16)
    low = (v - high.astype(jnp.float32)).astype(jnp.bfloat16)
    return high, low


def iota(shape, axis):
    return lax.broadcasted_iota(jnp.int32, shape, axis)


def dot(a, b):
    return jnp.dot(a, b, preferred_element_type=jnp.float32)


def layer_kernel(
    n_ep,
    n_kv,
    queries,
    key_pool,
    value_pool,
    page_table,
    lengths,
    prefill,
    residual,
    w_out,
    norm_gain,
    router,
    w_gate,
    w_up,
    w_down,
    final_gain,
    routes_t,
    out,
    kbuf,
    vbuf,
    wobuf,
    attn,
    pack_all,
    stat_all,
    scaled_all,
    hidden,
    code_t,
    pick_t,
    sends,
    arrived,
    gates,
    ups,
    downs,
    total,
    replies,
    returned,
    part_out,
    part_in,
    square_all,
    load_sem,
    pack_sem,
    stat_sem,
    scaled_sem,
    weight_send,
    weight_recv,
    onward_send,
    onward_recv,
    out_sem,
    back_sem,
    part_sem,
    square_sem,
):
    me = lax.axis_index("ep")
    q = lax.axis_index("kv")
    rows, cols = hidden.shape
    width = cols * n_kv
    requests = queries.shape[0]
    heads = width // HEAD_DIM
    experts, share = sends.shape[0], sends.shape[1]
    tokens = kbuf.shape[0]
    page_rows = tokens // (requests * page_table.shape[2])

    def peer(d):
        return {"kv": lax.rem(q + d, n_kv)}

    loads = [
        pltpu.make_async_copy(key_pool, kbuf, load_sem.at[0]),
        pltpu.make_async_copy(value_pool, vbuf, load_sem.at[1]),
        pltpu.make_async_copy(w_out, wobuf, load_sem.at[2]),
        pltpu.make_async_copy(w_gate.at[0], gates.at[0], load_sem.at[3]),
        pltpu.make_async_copy(w_up.at[0], ups.at[0], load_sem.at[4]),
        pltpu.make_async_copy(w_down.at[0], downs.at[0], load_sem.at[5]),
    ]
    for load in loads:
        load.start()

    barrier = pltpu.get_barrier_semaphore()

    def greet(i, carry):
        pl.semaphore_signal(
            barrier, inc=1, device_id={"ep": lax.rem(me + i, n_ep)}, device_id_type=MESH
        )
        return carry

    lax.fori_loop(1, n_ep, greet, 0)
    for d in range(1, n_kv):
        pl.semaphore_signal(barrier, inc=1, device_id=peer(d), device_id_type=MESH)
    pl.semaphore_wait(barrier, n_ep - 1 + n_kv - 1)

    pairs = ((w_gate, gates), (w_up, ups), (w_down, downs))

    def half(ref, slot, side):
        size = ref.shape[1] // 2
        return ref.at[slot, pl.ds(side * size, size)]

    def ring_copy(w, way, side):
        source, target = pairs[w]
        return pltpu.make_async_remote_copy(
            src_ref=half(source, 0, side),
            dst_ref=half(target, 1 + way, side),
            send_sem=weight_send.at[w, way, side],
            recv_sem=weight_recv.at[w, way, side],
            device_id=peer(1 if way == 0 else n_kv - 1),
            device_id_type=MESH,
        )

    def onward_copy(w, way):
        target = pairs[w][1]
        return pltpu.make_async_remote_copy(
            src_ref=half(target, 1 + way, way),
            dst_ref=half(target, 3, way),
            send_sem=onward_send.at[w, way],
            recv_sem=onward_recv.at[w, way],
            device_id=peer(1 if way == 0 else n_kv - 1),
            device_id_type=MESH,
        )

    def start_weights():
        for w in range(3):
            for turn in range(2):
                for way in range(2):
                    ring_copy(w, way, way ^ turn).start()

    start_weights()

    on_head = iota((heads, width), 1) // HEAD_DIM == iota((heads, width), 0)
    spread = jnp.concatenate(
        [
            jnp.where(on_head, queries[r : r + 1, :].astype(jnp.float32), 0.0)
            for r in range(requests)
        ],
        axis=0,
    ).astype(jnp.bfloat16)
    lane = iota((heads, tokens), 1)
    page_of, in_page = lane // page_rows, lane % page_rows
    seen = []
    for r in range(requests):
        place = jnp.full((heads, tokens), 1 << 30, jnp.int32)
        for j in range(page_table.shape[2]):
            first = (j * n_kv + q) * page_rows
            place = jnp.where(page_of == page_table[r, 0, j], first + in_page, place)
        seen.append((place < lengths[r]).astype(jnp.int32))
    visible = jnp.concatenate(seen, axis=0) > 0
    loads[0].wait()
    scores = lax.dot_general(
        spread, kbuf[...], (((1,), (1,)), ((), ())), preferred_element_type=jnp.float32
    ) * (1.0 / math.sqrt(HEAD_DIM))
    masked = jnp.where(visible, scores, floor_score)
    peak = jnp.max(masked, axis=1, keepdims=True)
    weights = jnp.where(visible, jnp.exp(masked - peak), 0.0)
    mass = jnp.sum(weights, axis=1, keepdims=True)
    high, low = split_two(weights)
    loads[1].wait()
    wide = dot(high, vbuf[...]) + dot(low, vbuf[...])

    def on_lanes(values, r):
        part = jnp.broadcast_to(values[r * heads : (r + 1) * heads], (heads, width))
        return jnp.sum(jnp.where(on_head, part, 0.0), axis=0, keepdims=True)

    for r in range(requests):
        for i, item in enumerate((wide, peak, mass)):
            pack_all[q, i * requests + r : i * requests + r + 1, :] = on_lanes(item, r)

    def exchange(ref, sems):
        copies = []
        for d in range(1, n_kv):
            copies.append(
                pltpu.make_async_remote_copy(
                    src_ref=ref.at[q],
                    dst_ref=ref.at[q],
                    send_sem=sems.at[0, d - 1],
                    recv_sem=sems.at[1, d - 1],
                    device_id=peer(d),
                    device_id_type=MESH,
                )
            )
            copies[-1].start()
        return copies

    pack_copies = exchange(pack_all, pack_sem)

    expert_of = iota((experts, rows), 0)
    named = jnp.zeros((experts, rows), jnp.float32)
    for k in range(TOP):
        named = jnp.where(expert_of == routes_t[k : k + 1, :], 1.0, named)
    before = (iota((rows, rows), 0) < iota((rows, rows), 1)).astype(jnp.float32)
    rank = dot(named.astype(jnp.bfloat16), before.astype(jnp.bfloat16))
    code_t[...] = jnp.where(named > 0, rank, -1.0).astype(jnp.int32)
    slot = q * share + iota((experts, share, rows), 1)
    pick = (code_t[...][:, None, :] == slot).astype(jnp.float32).reshape(experts * share, rows)
    pick_t[...] = pick.astype(jnp.bfloat16)

    loads[2].wait()
    attn[0 : prefill.shape[0], :] = prefill[...]
    for copy in pack_copies:
        copy.wait()
    packs = pack_all[...]
    sums = packs[:, 0:requests]
    peaks = packs[:, requests : 2 * requests]
    masses = packs[:, 2 * requests : 3 * requests]
    factors = jnp.exp(peaks - jnp.max(peaks, axis=0)[None])
    attn[prefill.shape[0] :, :] = (
        jnp.sum(sums * factors, axis=0) / jnp.sum(masses * factors, axis=0)
    ).astype(jnp.bfloat16)
    state = residual[...].astype(jnp.float32) + dot(attn[...], wobuf[...])
    hidden[...] = state
    scaled = (state * norm_gain[...]).astype(jnp.bfloat16)
    scaled_all[q] = scaled
    squares = jnp.sum(state * state, axis=1, keepdims=True)
    stat_all[q] = jnp.concatenate(
        [
            dot(scaled, router[...]),
            jnp.broadcast_to(squares, (rows, 128 - experts)),
        ],
        axis=1,
    )
    stat_copies = exchange(stat_all, stat_sem)
    scaled_copies = exchange(scaled_all, scaled_sem)
    for copy in stat_copies:
        copy.wait()
    stats = stat_all[0]
    for j in range(1, n_kv):
        stats = stats + stat_all[j]
    inv_first = lax.rsqrt(stats[:, experts : experts + 1] / width + epsilon)
    logits_t = (stats * inv_first).T[0:experts, :]
    raised = jnp.where(code_t[...] >= 0, jnp.exp(logits_t), 0.0)
    gate_t = raised / jnp.sum(raised, axis=0, keepdims=True)
    for copy in scaled_copies:
        copy.wait()
    for j in range(n_kv):
        normed = (scaled_all[j].astype(jnp.float32) * inv_first).astype(jnp.bfloat16)
        picked = dot(pick_t[...], normed).reshape(experts, share, cols)
        sends[:, :, j * cols : (j + 1) * cols] = picked.astype(jnp.bfloat16)

    def all_to_all(source, target, sems):
        def send(i, carry):
            other = lax.rem(me + i, n_ep)
            pltpu.make_async_remote_copy(
                src_ref=source.at[other],
                dst_ref=target.at[me],
                send_sem=sems.at[0],
                recv_sem=sems.at[1],
                device_id={"ep": other},
                device_id_type=MESH,
            ).start()
            return carry

        lax.fori_loop(1, n_ep, send, 0)
        own = pltpu.make_async_copy(source.at[me], target.at[me], sems.at[2])
        own.start()

        def finish():
            own.wait()
            rest = source.at[pl.ds(0, n_ep - 1)]
            pltpu.make_async_copy(rest, rest, sems.at[0]).wait()
            pltpu.make_async_copy(rest, rest, sems.at[1]).wait()

        return finish

    finish_out = all_to_all(sends, arrived, out_sem)

    for w in range(3):
        for way in range(2):
            ring_copy(w, way, way).wait_recv()
            onward_copy(w, way).start()
    mix_high, mix_low = split_two(
        (
            jnp.broadcast_to(gate_t[:, None, :], (experts, share, rows))
            .reshape(experts * share, rows)
            * pick_t[...].astype(jnp.float32)
        ).T
    )
    for w in range(3):
        loads[3 + w].wait()
        for way in range(2):
            ring_copy(w, way, 1 - way).wait_recv()

    finish_out()

    tile_blocks = 32
    tile_rows = tile_blocks * share
    wide_cols = 512

    def chunk(c):
        def tile(m, carry):
            block = pl.multiple_of(m * tile_blocks, tile_blocks)
            row = pl.multiple_of(m * tile_rows, tile_rows)
            x = arrived[pl.ds(block, tile_blocks)].reshape(tile_rows, width)
            g = dot(x, gates[c])
            u = dot(x, ups[c])
            act = (g / (1.0 + jnp.exp(-g)) * u).astype(jnp.bfloat16)
            for n in range(width // wide_cols):
                span = pl.ds(n * wide_cols, wide_cols)
                term = dot(act, downs[c, :, span])
                if c > 0:
                    term = term + total[pl.ds(row, tile_rows), span]
                if c < n_kv - 1:
                    total[pl.ds(row, tile_rows), span] = term
                else:
                    replies[pl.ds(block, tile_blocks), :, span] = term.reshape(
                        tile_blocks, share, wide_cols
                    ).astype(jnp.bfloat16)
            return carry

        lax.fori_loop(0, n_ep // tile_blocks, tile, 0)

    for c in range(n_kv - 1):
        chunk(c)
    for w in range(3):
        for way in range(2):
            onward_copy(w, way).wait_recv()
    chunk(n_kv - 1)

    finish_back = all_to_all(replies, returned, back_sem)
    for w in range(3):
        for way in range(2):
            for side in range(2):
                ring_copy(w, way, side).wait_send()
            onward_copy(w, way).wait_send()
    finish_back()

    for j in range(n_kv):
        span = pl.ds(j * cols, cols)
        back = returned[:, :, span].reshape(experts * share, cols)
        part_out[j] = (dot(mix_high, back) + dot(mix_low, back)).astype(jnp.bfloat16)
    part_copies = []
    for d in range(1, n_kv):
        part_copies.append(
            pltpu.make_async_remote_copy(
                src_ref=part_out.at[lax.rem(q + d, n_kv)],
                dst_ref=part_in.at[d - 1],
                send_sem=part_sem.at[0, d - 1],
                recv_sem=part_sem.at[1, d - 1],
                device_id=peer(d),
                device_id_type=MESH,
            )
        )
        part_copies[-1].start()
    combined = hidden[...] + part_out[q].astype(jnp.float32)
    for copy in part_copies:
        copy.wait()
    for d in range(1, n_kv):
        combined = combined + part_in[d - 1].astype(jnp.float32)
    own_square = jnp.sum(combined * combined, axis=1, keepdims=True)
    square_all[q] = jnp.broadcast_to(own_square, (rows, 128))
    for copy in exchange(square_all, square_sem):
        copy.wait()
    square = square_all[0]
    for j in range(1, n_kv):
        square = square + square_all[j]
    inv_second = lax.rsqrt(square[:, 0:1] / width + epsilon)
    out[...] = (combined * inv_second * final_gain[...]).astype(out.dtype)


def make_per_device(n_ep, n_kv):
    def per_device(
        queries,
        key_pool,
        value_pool,
        page_table,
        lengths,
        prefill_attn,
        residual,
        w_out,
        norm_gain,
        router,
        w_gate,
        w_up,
        w_down,
        final_gain,
        routes,
    ):
        width = queries.shape[1]
        rows, cols = residual.shape
        experts = router.shape[1]
        share = min(rows, 2 * rows * TOP // experts) // n_kv
        tokens = key_pool.shape[0] * key_pool.shape[1]
        packed = 3 * queries.shape[0]
        f32, bf16 = jnp.float32, jnp.bfloat16
        vmem = pl.BlockSpec(memory_space=pltpu.VMEM)
        smem = pl.BlockSpec(memory_space=pltpu.SMEM)
        anywhere = pl.BlockSpec(memory_space=pl.ANY)
        dma = pltpu.SemaphoreType.DMA
        return pl.pallas_call(
            lambda *refs: layer_kernel(n_ep, n_kv, *refs),
            name="layer",
            out_shape=jax.ShapeDtypeStruct((rows, cols), bf16),
            in_specs=[vmem, anywhere, anywhere, smem, smem, vmem, vmem, anywhere, vmem, vmem]
            + [anywhere] * 3
            + [vmem, vmem],
            out_specs=vmem,
            scratch_shapes=[
                pltpu.VMEM((tokens, width), bf16),
                pltpu.VMEM((tokens, width), bf16),
                pltpu.VMEM(w_out.shape, bf16),
                pltpu.VMEM((rows, width), bf16),
                pltpu.VMEM((n_kv, packed, width), f32),
                pltpu.VMEM((n_kv, rows, 128), f32),
                pltpu.VMEM((n_kv, rows, cols), bf16),
                pltpu.VMEM((rows, cols), f32),
                pltpu.VMEM((experts, rows), jnp.int32),
                pltpu.VMEM((experts * share, rows), bf16),
                pltpu.VMEM((experts, share, width), bf16),
                pltpu.VMEM((experts, share, width), bf16),
                pltpu.VMEM((n_kv,) + w_gate.shape[1:], bf16),
                pltpu.VMEM((n_kv,) + w_up.shape[1:], bf16),
                pltpu.VMEM((n_kv,) + w_down.shape[1:], bf16),
                pltpu.VMEM((experts * share, width), f32),
                pltpu.VMEM((experts, share, width), bf16),
                pltpu.VMEM((experts, share, width), bf16),
                pltpu.VMEM((n_kv, rows, cols), bf16),
                pltpu.VMEM((n_kv - 1, rows, cols), bf16),
                pltpu.VMEM((n_kv, rows, 128), f32),
                dma((6,)),
                dma((2, n_kv - 1)),
                dma((2, n_kv - 1)),
                dma((2, n_kv - 1)),
                dma((3, 2, 2)),
                dma((3, 2, 2)),
                dma((3, 2)),
                dma((3, 2)),
                dma((3,)),
                dma((3,)),
                dma((2, n_kv - 1)),
                dma((2, n_kv - 1)),
            ],
            compiler_params=pltpu.CompilerParams(
                collective_id=0, has_side_effects=True, vmem_limit_bytes=60 << 20
            ),
        )(
            queries,
            key_pool.reshape(tokens, width),
            value_pool.reshape(tokens, width),
            page_table,
            lengths,
            prefill_attn,
            residual,
            w_out,
            norm_gain.reshape(1, cols),
            router,
            w_gate,
            w_up,
            w_down,
            final_gain.reshape(1, cols),
            routes.T,
        )

    return per_device


def solution(mesh):
    placed = (
        P("ep", None),
        P(("ep", "kv"), None, None),
        P(("ep", "kv"), None, None),
        P("ep", "kv", None),
        P("ep"),
        P("ep", None),
        P("ep", "kv"),
        P(None, "kv"),
        P("kv"),
        P("kv", None),
        P("ep", None, "kv"),
        P("ep", None, "kv"),
        P("ep", "kv", None),
        P("kv"),
        P("ep", None),
    )
    return jax.shard_map(
        make_per_device(mesh.shape["ep"], mesh.shape["kv"]),
        mesh=mesh,
        in_specs=placed,
        out_specs=P("ep", "kv"),
        check_vma=False,
    )
```

```python
import math

import jax
import jax.numpy as jnp
from jax import lax
from jax.experimental import pallas as pl
from jax.experimental.pallas import tpu as pltpu
from jax.sharding import PartitionSpec as P

HEAD_DIM = 128
TOP = 8

epsilon = 1e-06
floor_score = -1e30
MESH = pl.DeviceIdType.MESH
PACE = (1, 2)


def split_two(v):
    high = v.astype(jnp.bfloat16)
    low = (v - high.astype(jnp.float32)).astype(jnp.bfloat16)
    return high, low


def iota(shape, axis):
    return lax.broadcasted_iota(jnp.int32, shape, axis)


def dot(a, b):
    return jnp.dot(a, b, preferred_element_type=jnp.float32)


def layer_kernel(
    n_ep,
    n_kv,
    queries,
    key_pool,
    value_pool,
    page_table,
    lengths,
    prefill,
    residual,
    w_out,
    norm_gain,
    router_t,
    w_gate,
    w_up,
    w_down,
    final_gain,
    routes_t,
    out,
    kbuf,
    vbuf,
    wobuf,
    attn,
    pack_all,
    stat_all,
    scaled_all,
    hidden,
    code_t,
    pick_t,
    sends,
    arrived,
    gates,
    ups,
    downs,
    acts,
    replies,
    returned,
    part_out,
    part_in,
    square_all,
    load_sem,
    pack_sem,
    stat_sem,
    scaled_sem,
    weight_sem,
    onward_sem,
    down_sem,
    down_onward_sem,
    out_sem,
    back_sem,
    part_sem,
    square_sem,
):
    me = lax.axis_index("ep")
    q = lax.axis_index("kv")
    rows, cols = hidden.shape
    width = cols * n_kv
    requests = queries.shape[0]
    heads = width // HEAD_DIM
    experts, share = sends.shape[1], sends.shape[2]
    tokens = kbuf.shape[0]
    page_rows = tokens // (requests * page_table.shape[2])

    def peer(d):
        return {"kv": lax.rem(q + d, n_kv)}

    loads = [
        pltpu.make_async_copy(key_pool, kbuf, load_sem.at[0]),
        pltpu.make_async_copy(value_pool, vbuf, load_sem.at[1]),
        pltpu.make_async_copy(w_out, wobuf, load_sem.at[2]),
        pltpu.make_async_copy(w_gate.at[0], gates.at[0], load_sem.at[3]),
        pltpu.make_async_copy(w_up.at[0], ups.at[0], load_sem.at[4]),
        pltpu.make_async_copy(w_down.at[0], downs.at[0], load_sem.at[5]),
    ]
    for load in loads:
        load.start()

    barrier = pltpu.get_barrier_semaphore()

    def greet(i, carry):
        pl.semaphore_signal(
            barrier, inc=1, device_id={"ep": lax.rem(me + i, n_ep)}, device_id_type=MESH
        )
        return carry

    lax.fori_loop(1, n_ep, greet, 0)
    for d in range(1, n_kv):
        pl.semaphore_signal(barrier, inc=1, device_id=peer(d), device_id_type=MESH)

    on_head = iota((heads, width), 1) // HEAD_DIM == iota((heads, width), 0)
    spread = jnp.concatenate(
        [
            jnp.where(on_head, queries[r : r + 1, :].astype(jnp.float32), 0.0)
            for r in range(requests)
        ],
        axis=0,
    ).astype(jnp.bfloat16)
    lane = iota((heads, tokens), 1)
    page_of, in_page = lane // page_rows, lane % page_rows
    seen = []
    for r in range(requests):
        place = jnp.full((heads, tokens), 1 << 30, jnp.int32)
        for j in range(page_table.shape[2]):
            first = (j * n_kv + q) * page_rows
            place = jnp.where(page_of == page_table[r, 0, j], first + in_page, place)
        seen.append((place < lengths[r]).astype(jnp.int32))
    visible = jnp.concatenate(seen, axis=0) > 0
    loads[0].wait()
    scores = lax.dot_general(
        spread, kbuf[...], (((1,), (1,)), ((), ())), preferred_element_type=jnp.float32
    ) * (1.0 / math.sqrt(HEAD_DIM))
    masked = jnp.where(visible, scores, floor_score)
    peak = jnp.max(masked, axis=1, keepdims=True)
    weights = jnp.where(visible, jnp.exp(masked - peak), 0.0)
    mass = jnp.sum(weights, axis=1, keepdims=True)
    high, low = split_two(weights)
    loads[1].wait()
    wide = dot(high, vbuf[...]) + dot(low, vbuf[...])

    def on_lanes(values, r):
        part = jnp.broadcast_to(values[r * heads : (r + 1) * heads], (heads, width))
        return jnp.sum(jnp.where(on_head, part, 0.0), axis=0, keepdims=True)

    for r in range(requests):
        for i, item in enumerate((wide, peak, mass)):
            pack_all[q, i * requests + r : i * requests + r + 1, :] = on_lanes(item, r)

    pl.semaphore_wait(barrier, n_ep - 1 + n_kv - 1)

    def exchange(ref, sems):
        copies = []
        for d in range(1, n_kv):
            copies.append(
                pltpu.make_async_remote_copy(
                    src_ref=ref.at[q],
                    dst_ref=ref.at[q],
                    send_sem=sems.at[0, d - 1],
                    recv_sem=sems.at[1, d - 1],
                    device_id=peer(d),
                    device_id_type=MESH,
                )
            )
            copies[-1].start()
        return copies

    pack_copies = exchange(pack_all, pack_sem)

    pairs = ((w_gate, gates), (w_up, ups))
    piece = gates.shape[1] // 4
    down_rows = downs.shape[1] // 2

    def neighbour(way):
        return peer(1 if way == 0 else n_kv - 1)

    def ring_copy(w, way, part):
        source, target = pairs[w]
        return pltpu.make_async_remote_copy(
            src_ref=source.at[0, pl.ds(part * piece, piece)],
            dst_ref=target.at[1 + way, pl.ds(part * piece, piece)],
            send_sem=weight_sem.at[0, w, way, part],
            recv_sem=weight_sem.at[1, w, way, part],
            device_id=neighbour(way),
            device_id_type=MESH,
        )

    def onward_copy(w, way, k):
        target = pairs[w][1]
        span = pl.ds((2 * way + k) * piece, piece)
        return pltpu.make_async_remote_copy(
            src_ref=target.at[1 + way, span],
            dst_ref=target.at[3, span],
            send_sem=onward_sem.at[0, w, way, k],
            recv_sem=onward_sem.at[1, w, way, k],
            device_id=neighbour(way),
            device_id_type=MESH,
        )

    def down_copy(n, way):
        span = pl.ds(n * cols, cols)
        return pltpu.make_async_remote_copy(
            src_ref=w_down.at[0, :, span],
            dst_ref=downs.at[1 + way, :, span],
            send_sem=down_sem.at[0, n, way],
            recv_sem=down_sem.at[1, n, way],
            device_id=neighbour(way),
            device_id_type=MESH,
        )

    def down_onward(n, way):
        span = pl.ds(n * cols, cols)
        some = pl.ds(way * down_rows, down_rows)
        return pltpu.make_async_remote_copy(
            src_ref=downs.at[1 + way, some, span],
            dst_ref=downs.at[3, some, span],
            send_sem=down_onward_sem.at[0, n, way],
            recv_sem=down_onward_sem.at[1, n, way],
            device_id=neighbour(way),
            device_id_type=MESH,
        )

    steps = [(w, k) for w in range(2) for k in range(4)]

    def start_steps(first, last):
        for w, k in steps[first:last]:
            for way in range(2):
                ring_copy(w, way, (k + 2 * way) % 4).start()

    start_steps(0, PACE[0])

    expert_of = iota((experts, rows), 0)
    named = jnp.zeros((experts, rows), jnp.float32)
    for k in range(TOP):
        named = jnp.where(expert_of == routes_t[k : k + 1, :], 1.0, named)
    before = (iota((rows, rows), 0) < iota((rows, rows), 1)).astype(jnp.float32)
    rank = dot(named.astype(jnp.bfloat16), before.astype(jnp.bfloat16))
    code_t[...] = jnp.where(named > 0, rank, -1.0).astype(jnp.int32)
    slot = q * share + iota((experts, share, rows), 1)
    pick = (code_t[...][:, None, :] == slot).astype(jnp.float32).reshape(experts * share, rows)
    pick_t[...] = pick.astype(jnp.bfloat16)

    loads[2].wait()
    attn[0 : prefill.shape[0], :] = prefill[...]
    for copy in pack_copies:
        copy.wait()
    packs = pack_all[...]
    sums = packs[:, 0:requests]
    peaks = packs[:, requests : 2 * requests]
    masses = packs[:, 2 * requests : 3 * requests]
    factors = jnp.exp(peaks - jnp.max(peaks, axis=0)[None])
    attn[prefill.shape[0] :, :] = (
        jnp.sum(sums * factors, axis=0) / jnp.sum(masses * factors, axis=0)
    ).astype(jnp.bfloat16)
    state = residual[...].astype(jnp.float32) + dot(attn[...], wobuf[...])
    hidden[...] = state
    scaled = (state * norm_gain[...]).astype(jnp.bfloat16)
    scaled_all[q] = scaled
    squares = jnp.sum(state * state, axis=1, keepdims=True)
    scores_of = lax.dot_general(
        scaled, router_t[...], (((1,), (1,)), ((), ())), preferred_element_type=jnp.float32
    )
    stat = jnp.concatenate([scores_of, jnp.broadcast_to(squares, (rows, 128 - experts))], axis=1)
    stat_all[q] = stat.T[0 : stat_all.shape[1], :]
    stat_copies = exchange(stat_all, stat_sem)
    scaled_copies = exchange(scaled_all, scaled_sem)
    start_steps(PACE[0], PACE[1])
    for copy in stat_copies:
        copy.wait()
    stats = stat_all[0]
    for j in range(1, n_kv):
        stats = stats + stat_all[j]
    inv_t = lax.rsqrt(stats[experts : experts + 1, :] / width + epsilon)
    inv_first = jnp.broadcast_to(inv_t, (128, rows)).T[:, 0:1]

    def all_to_all(source, target, sems):
        def send(i, carry):
            other = lax.rem(me + i, n_ep)
            pltpu.make_async_remote_copy(
                src_ref=source.at[other],
                dst_ref=target.at[me],
                send_sem=sems.at[0],
                recv_sem=sems.at[1],
                device_id={"ep": other},
                device_id_type=MESH,
            ).start()
            return carry

        lax.fori_loop(1, n_ep, send, 0)
        own = pltpu.make_async_copy(source.at[me], target.at[me], sems.at[2])
        own.start()

        def received():
            own.wait()
            rest = target.at[pl.ds(0, n_ep - 1)]
            pltpu.make_async_copy(rest, rest, sems.at[1]).wait()

        def sent():
            rest = source.at[pl.ds(0, n_ep - 1)]
            pltpu.make_async_copy(rest, rest, sems.at[0]).wait()

        return received, sent

    order = (0, 3, 1, 2)
    out_waits = []
    for i, off in enumerate(order):
        if i > 0:
            scaled_copies[n_kv - off - 1].wait()
        quarter = scaled_all[lax.rem(q + off, n_kv)]
        normed = (quarter.astype(jnp.float32) * inv_first).astype(jnp.bfloat16)
        picked = dot(pick_t[...], normed).reshape(experts, share, cols)
        sends[i] = picked.astype(jnp.bfloat16)
        out_waits.append(all_to_all(sends.at[i], arrived.at[i], out_sem.at[i]))

    start_steps(PACE[1], len(steps))
    for w in range(2):
        for k in range(2):
            for way in range(2):
                ring_copy(w, way, 2 * way + k).wait_recv()
                onward_copy(w, way, k).start()
    for n in range(2):
        for way in range(2):
            down_copy(n, way).start()
    logits_t = stats[0:experts, :] * inv_t
    raised = jnp.where(code_t[...] >= 0, jnp.exp(logits_t), 0.0)
    gate_t = raised / jnp.sum(raised, axis=0, keepdims=True)
    mix_high, mix_low = split_two(
        (
            jnp.broadcast_to(gate_t[:, None, :], (experts, share, rows))
            .reshape(experts * share, rows)
            * pick_t[...].astype(jnp.float32)
        ).T
    )
    for w in range(3):
        loads[3 + w].wait()
    for w in range(2):
        for k in range(2):
            for way in range(2):
                ring_copy(w, way, 2 * (1 - way) + k).wait_recv()
    for received, _ in out_waits:
        received()

    tile_blocks = 32
    tile_rows = tile_blocks * share

    def expert_in(c):
        def tile(m, carry):
            block = pl.multiple_of(m * tile_blocks, tile_blocks)
            row = pl.multiple_of(m * tile_rows, tile_rows)
            g = jnp.zeros((tile_rows, gates.shape[2]), jnp.float32)
            u = jnp.zeros((tile_rows, gates.shape[2]), jnp.float32)
            for i, off in enumerate(order):
                x = arrived[i, pl.ds(block, tile_blocks)].reshape(tile_rows, cols)
                some = pl.ds(pl.multiple_of(lax.rem(q + off, n_kv) * cols, cols), cols)
                g = g + dot(x, gates[c, some, :])
                u = u + dot(x, ups[c, some, :])
            acts[c, pl.ds(row, tile_rows), :] = (g / (1.0 + jnp.exp(-g)) * u).astype(jnp.bfloat16)
            return carry

        lax.fori_loop(0, n_ep // tile_blocks, tile, 0)

    def expert_out(n):
        span = pl.ds(n * cols, cols)

        def tile(m, carry):
            block = pl.multiple_of(m * tile_blocks, tile_blocks)
            row = pl.multiple_of(m * tile_rows, tile_rows)
            term = jnp.zeros((tile_rows, cols), jnp.float32)
            for c in range(n_kv):
                term = term + dot(acts[c, pl.ds(row, tile_rows), :], downs[c, :, span])
            replies[n, pl.ds(block, tile_blocks)] = term.reshape(
                tile_blocks, share, cols
            ).astype(jnp.bfloat16)
            return carry

        lax.fori_loop(0, n_ep // tile_blocks, tile, 0)

    def advance(n):
        for way in range(2):
            down_copy(n, way).wait_recv()
            down_onward(n, way).start()
            if n + 2 < n_kv:
                down_copy(n + 2, way).start()

    for c in range(n_kv - 1):
        expert_in(c)
    advance(0)
    for w in range(2):
        for k in range(2):
            for way in range(2):
                onward_copy(w, way, k).wait_recv()
    expert_in(n_kv - 1)
    back_waits = []
    for n in range(n_kv):
        if n + 1 < n_kv:
            advance(n + 1)
        for way in range(2):
            down_onward(n, way).wait_recv()
        expert_out(n)
        back_waits.append(all_to_all(replies.at[n], returned.at[n], back_sem.at[n]))
    for _, sent in out_waits:
        sent()
    for w in range(2):
        for way in range(2):
            for part in range(4):
                ring_copy(w, way, part).wait_send()
            for k in range(2):
                onward_copy(w, way, k).wait_send()
    for n in range(n_kv):
        for way in range(2):
            down_copy(n, way).wait_send()
            down_onward(n, way).wait_send()

    def part_copy(n):
        place = lax.rem(q - n + n_kv, n_kv) - 1
        return pltpu.make_async_remote_copy(
            src_ref=part_out.at[n],
            dst_ref=part_in.at[place],
            send_sem=part_sem.at[0, n],
            recv_sem=part_sem.at[1, place],
            device_id={"kv": n},
            device_id_type=MESH,
        )

    for n in range(n_kv):
        back_waits[n][0]()
        back = returned[n].reshape(experts * share, cols)
        part_out[n] = (dot(mix_high, back) + dot(mix_low, back)).astype(jnp.bfloat16)

        @pl.when(q != n)
        def _():
            part_copy(n).start()

    combined = hidden[...] + part_out[q].astype(jnp.float32)
    for d in range(1, n_kv):
        pltpu.make_async_copy(part_in.at[d - 1], part_in.at[d - 1], part_sem.at[1, d - 1]).wait()
        combined = combined + part_in[d - 1].astype(jnp.float32)
    own_square = jnp.sum(combined * combined, axis=1, keepdims=True)
    square_all[q] = jnp.broadcast_to(own_square, (rows, 128)).T[0:8, :]
    square_copies = exchange(square_all, square_sem)
    for _, sent in back_waits:
        sent()
    for n in range(n_kv):

        @pl.when(q != n)
        def _():
            part_copy(n).wait_send()

    for copy in square_copies:
        copy.wait()
    square = square_all[0]
    for j in range(1, n_kv):
        square = square + square_all[j]
    inv_row = lax.rsqrt(square[0:1] / width + epsilon)
    inv_second = jnp.broadcast_to(inv_row, (128, rows)).T[:, 0:1]
    out[...] = (combined * inv_second * final_gain[...]).astype(out.dtype)


def make_per_device(n_ep, n_kv):
    def per_device(
        queries,
        key_pool,
        value_pool,
        page_table,
        lengths,
        prefill_attn,
        residual,
        w_out,
        norm_gain,
        router,
        w_gate,
        w_up,
        w_down,
        final_gain,
        routes,
    ):
        width = queries.shape[1]
        rows, cols = residual.shape
        experts = router.shape[1]
        share = min(rows, 2 * rows * TOP // experts) // n_kv
        tokens = key_pool.shape[0] * key_pool.shape[1]
        packed = 3 * queries.shape[0]
        f32, bf16 = jnp.float32, jnp.bfloat16
        vmem = pl.BlockSpec(memory_space=pltpu.VMEM)
        smem = pl.BlockSpec(memory_space=pltpu.SMEM)
        anywhere = pl.BlockSpec(memory_space=pl.ANY)
        dma = pltpu.SemaphoreType.DMA
        return pl.pallas_call(
            lambda *refs: layer_kernel(n_ep, n_kv, *refs),
            name="layer",
            out_shape=jax.ShapeDtypeStruct((rows, cols), bf16),
            in_specs=[vmem, anywhere, anywhere, smem, smem, vmem, vmem, anywhere, vmem, vmem]
            + [anywhere] * 3
            + [vmem, vmem],
            out_specs=vmem,
            scratch_shapes=[
                pltpu.VMEM((tokens, width), bf16),
                pltpu.VMEM((tokens, width), bf16),
                pltpu.VMEM(w_out.shape, bf16),
                pltpu.VMEM((rows, width), bf16),
                pltpu.VMEM((n_kv, packed, width), f32),
                pltpu.VMEM((n_kv, experts + 8, rows), f32),
                pltpu.VMEM((n_kv, rows, cols), bf16),
                pltpu.VMEM((rows, cols), f32),
                pltpu.VMEM((experts, rows), jnp.int32),
                pltpu.VMEM((experts * share, rows), bf16),
                pltpu.VMEM((n_kv, experts, share, cols), bf16),
                pltpu.VMEM((n_kv, experts, share, cols), bf16),
                pltpu.VMEM((n_kv,) + w_gate.shape[1:], bf16),
                pltpu.VMEM((n_kv,) + w_up.shape[1:], bf16),
                pltpu.VMEM((n_kv,) + w_down.shape[1:], bf16),
                pltpu.VMEM((n_kv, experts * share, w_gate.shape[2]), bf16),
                pltpu.VMEM((n_kv, experts, share, cols), bf16),
                pltpu.VMEM((n_kv, experts, share, cols), bf16),
                pltpu.VMEM((n_kv, rows, cols), bf16),
                pltpu.VMEM((n_kv - 1, rows, cols), bf16),
                pltpu.VMEM((n_kv, 8, rows), f32),
                dma((6,)),
                dma((2, n_kv - 1)),
                dma((2, n_kv - 1)),
                dma((2, n_kv - 1)),
                dma((2, 2, 2, 4)),
                dma((2, 2, 2, 2)),
                dma((2, n_kv, 2)),
                dma((2, n_kv, 2)),
                dma((n_kv, 3)),
                dma((n_kv, 3)),
                dma((2, n_kv)),
                dma((2, n_kv - 1)),
            ],
            compiler_params=pltpu.CompilerParams(
                collective_id=0, has_side_effects=True, vmem_limit_bytes=60 << 20
            ),
        )(
            queries,
            key_pool.reshape(tokens, width),
            value_pool.reshape(tokens, width),
            page_table,
            lengths,
            prefill_attn,
            residual,
            w_out,
            norm_gain.reshape(1, cols),
            router.T,
            w_gate,
            w_up,
            w_down,
            final_gain.reshape(1, cols),
            routes.T,
        )

    return per_device


def solution(mesh):
    placed = (
        P("ep", None),
        P(("ep", "kv"), None, None),
        P(("ep", "kv"), None, None),
        P("ep", "kv", None),
        P("ep"),
        P("ep", None),
        P("ep", "kv"),
        P(None, "kv"),
        P("kv"),
        P("kv", None),
        P("ep", None, "kv"),
        P("ep", None, "kv"),
        P("ep", "kv", None),
        P("kv"),
        P("ep", None),
    )
    return jax.shard_map(
        make_per_device(mesh.shape["ep"], mesh.shape["kv"]),
        mesh=mesh,
        in_specs=placed,
        out_specs=P("ep", "kv"),
        check_vma=False,
    )
```

```python
import math

import jax
import jax.numpy as jnp
from jax import lax
from jax.experimental import pallas as pl
from jax.experimental.pallas import tpu as pltpu
from jax.sharding import PartitionSpec as P

HEAD_DIM = 128
TOP = 8

epsilon = 1e-06
floor_score = -1e30
MESH = pl.DeviceIdType.MESH


def split_two(v):
    high = v.astype(jnp.bfloat16)
    low = (v - high.astype(jnp.float32)).astype(jnp.bfloat16)
    return high, low


def iota(shape, axis):
    return lax.broadcasted_iota(jnp.int32, shape, axis)


def dot(a, b):
    return jnp.dot(a, b, preferred_element_type=jnp.float32)


def layer_kernel(
    n_ep,
    n_kv,
    queries,
    key_pool,
    value_pool,
    page_table,
    lengths,
    prefill,
    residual,
    w_out,
    norm_gain,
    router_t,
    w_gate,
    w_up,
    w_down,
    final_gain,
    routes_t,
    out,
    kbuf,
    vbuf,
    wobuf,
    attn,
    pack_all,
    stat_all,
    scaled_all,
    hidden,
    code_t,
    pick_t,
    sends,
    arrived,
    gates,
    ups,
    downs,
    acts,
    replies,
    returned,
    part_out,
    part_in,
    square_all,
    load_sem,
    pack_sem,
    stat_sem,
    scaled_sem,
    ring_sem,
    out_sem,
    back_sem,
    part_sem,
    square_sem,
):
    me = lax.axis_index("ep")
    q = lax.axis_index("kv")
    rows, cols = hidden.shape
    width = cols * n_kv
    requests = queries.shape[0]
    heads = width // HEAD_DIM
    experts, share = sends.shape[1], sends.shape[2]
    tokens = kbuf.shape[0]
    page_rows = tokens // (requests * page_table.shape[2])

    def peer(d):
        return {"kv": lax.rem(q + d, n_kv)}

    side = q // 2
    core = lax.rem(me, 2)
    home = core == side
    sibling = {"ep": me + 1 - 2 * core}
    partner = {"kv": q + 1 - 2 * lax.rem(q, 2)}
    across = {"kv": n_kv - 1 - q, "ep": me + 1 - 2 * core}

    loads = [
        pltpu.make_async_copy(key_pool, kbuf, load_sem.at[0]),
        pltpu.make_async_copy(value_pool, vbuf, load_sem.at[1]),
        pltpu.make_async_copy(w_out, wobuf, load_sem.at[2]),
    ]
    for load in loads:
        load.start()
    own_loads = [
        pltpu.make_async_copy(w_gate.at[0], gates.at[0], load_sem.at[3]),
        pltpu.make_async_copy(w_up.at[0], ups.at[0], load_sem.at[4]),
        pltpu.make_async_copy(w_down.at[0], downs.at[0], load_sem.at[5]),
    ]

    @pl.when(home)
    def _():
        for load in own_loads:
            load.start()

    barrier = pltpu.get_barrier_semaphore()

    def greet(i, carry):
        pl.semaphore_signal(
            barrier, inc=1, device_id={"ep": lax.rem(me + i, n_ep)}, device_id_type=MESH
        )
        return carry

    lax.fori_loop(1, n_ep, greet, 0)
    for d in range(1, n_kv):
        pl.semaphore_signal(barrier, inc=1, device_id=peer(d), device_id_type=MESH)
    pl.semaphore_signal(barrier, inc=1, device_id=across, device_id_type=MESH)

    on_head = iota((heads, width), 1) // HEAD_DIM == iota((heads, width), 0)
    spread = jnp.concatenate(
        [
            jnp.where(on_head, queries[r : r + 1, :].astype(jnp.float32), 0.0)
            for r in range(requests)
        ],
        axis=0,
    ).astype(jnp.bfloat16)
    lane = iota((heads, tokens), 1)
    page_of, in_page = lane // page_rows, lane % page_rows
    seen = []
    for r in range(requests):
        place = jnp.full((heads, tokens), 1 << 30, jnp.int32)
        for j in range(page_table.shape[2]):
            first = (j * n_kv + q) * page_rows
            place = jnp.where(page_of == page_table[r, 0, j], first + in_page, place)
        seen.append((place < lengths[r]).astype(jnp.int32))
    visible = jnp.concatenate(seen, axis=0) > 0
    loads[0].wait()
    scores = lax.dot_general(
        spread, kbuf[...], (((1,), (1,)), ((), ())), preferred_element_type=jnp.float32
    ) * (1.0 / math.sqrt(HEAD_DIM))
    masked = jnp.where(visible, scores, floor_score)
    peak = jnp.max(masked, axis=1, keepdims=True)
    weights = jnp.where(visible, jnp.exp(masked - peak), 0.0)
    mass = jnp.sum(weights, axis=1, keepdims=True)
    high, low = split_two(weights)
    loads[1].wait()
    wide = dot(high, vbuf[...]) + dot(low, vbuf[...])

    def on_lanes(values, r):
        part = jnp.broadcast_to(values[r * heads : (r + 1) * heads], (heads, width))
        return jnp.sum(jnp.where(on_head, part, 0.0), axis=0, keepdims=True)

    for r in range(requests):
        for i, item in enumerate((wide, peak, mass)):
            pack_all[q, i * requests + r : i * requests + r + 1, :] = on_lanes(item, r)

    pl.semaphore_wait(barrier, n_ep - 1 + n_kv)

    def exchange(ref, sems):
        copies = []
        for d in range(1, n_kv):
            copies.append(
                pltpu.make_async_remote_copy(
                    src_ref=ref.at[q],
                    dst_ref=ref.at[q],
                    send_sem=sems.at[0, d - 1],
                    recv_sem=sems.at[1, d - 1],
                    device_id=peer(d),
                    device_id_type=MESH,
                )
            )
            copies[-1].start()
        return copies

    pack_copies = exchange(pack_all, pack_sem)

    piece = gates.shape[1] // 4
    wide_items, items = 8, 12

    def view(slot, t):
        if t < wide_items:
            return (gates, ups)[t // 4].at[slot, pl.ds(t % 4 * piece, piece)]
        return downs.at[slot, :, pl.ds((t - wide_items) * cols, cols)]

    def own_view(t):
        if t < wide_items:
            return (w_gate, w_up)[t // 4].at[0, pl.ds(t % 4 * piece, piece)]
        return w_down.at[0, :, pl.ds((t - wide_items) * cols, cols)]

    def move(kind, t):
        source, slot, device = (
            (own_view(t), 0, across),
            (view(0, t), 1, partner),
            (view(0, t), 2, sibling),
            (view(1, t), 3, sibling),
        )[kind]
        return pltpu.make_async_remote_copy(
            src_ref=source,
            dst_ref=view(slot, t),
            send_sem=ring_sem.at[0, kind, t],
            recv_sem=ring_sem.at[1, kind, t],
            device_id=device,
            device_id_type=MESH,
        )

    def first_on(t):
        move(1, t).start()
        move(2, t).start()

    def second_on(t):
        move(1, t).wait_recv()
        move(3, t).start()

    def pump(home_items, cross_items, guest_items):
        @pl.when(home)
        def _():
            for t in home_items:
                first_on(t)

        @pl.when(jnp.logical_not(home))
        def _():
            for t in cross_items:
                move(0, t).start()
            for t in guest_items:
                move(0, t).wait_recv()
                first_on(t)

    @pl.when(home)
    def _():
        for load in own_loads:
            load.wait()

    pump(range(0, 1), range(0, 2), ())

    def naming(expert_of):
        named = jnp.zeros((experts, rows), jnp.float32)
        for k in range(TOP):
            named = jnp.where(expert_of == routes_t[k : k + 1, :], 1.0, named)
        return named

    device_of = iota((experts, rows), 0)
    named = naming(device_of // 2 * 2 + side)
    before = (iota((rows, rows), 0) < iota((rows, rows), 1)).astype(jnp.float32)
    rank = dot(named.astype(jnp.bfloat16), before.astype(jnp.bfloat16))
    code_t[...] = jnp.where(named > 0, rank, -1.0).astype(jnp.int32)
    slot = (lax.rem(q, 2) * 2 + iota((experts, share, rows), 0) % 2) * share + iota(
        (experts, share, rows), 1
    )
    pick = (code_t[...][:, None, :] == slot).astype(jnp.float32).reshape(experts * share, rows)
    pick_t[...] = pick.astype(jnp.bfloat16)

    loads[2].wait()
    attn[0 : prefill.shape[0], :] = prefill[...]
    for copy in pack_copies:
        copy.wait()
    packs = pack_all[...]
    sums = packs[:, 0:requests]
    peaks = packs[:, requests : 2 * requests]
    masses = packs[:, 2 * requests : 3 * requests]
    factors = jnp.exp(peaks - jnp.max(peaks, axis=0)[None])
    attn[prefill.shape[0] :, :] = (
        jnp.sum(sums * factors, axis=0) / jnp.sum(masses * factors, axis=0)
    ).astype(jnp.bfloat16)
    state = residual[...].astype(jnp.float32) + dot(attn[...], wobuf[...])
    hidden[...] = state
    scaled = (state * norm_gain[...]).astype(jnp.bfloat16)
    scaled_all[q] = scaled
    squares = jnp.sum(state * state, axis=1, keepdims=True)
    scores_of = lax.dot_general(
        scaled, router_t[...], (((1,), (1,)), ((), ())), preferred_element_type=jnp.float32
    )
    stat = jnp.concatenate([scores_of, jnp.broadcast_to(squares, (rows, 128 - experts))], axis=1)
    stat_all[q] = stat.T[0 : stat_all.shape[1], :]
    stat_copies = exchange(stat_all, stat_sem)
    scaled_copies = exchange(scaled_all, scaled_sem)
    pump(range(1, 3), range(2, 3), range(0, 1))
    for copy in stat_copies:
        copy.wait()
    stats = stat_all[0]
    for j in range(1, n_kv):
        stats = stats + stat_all[j]
    inv_t = lax.rsqrt(stats[experts : experts + 1, :] / width + epsilon)
    inv_first = jnp.broadcast_to(inv_t, (128, rows)).T[:, 0:1]

    def all_to_all(source, target, sems):
        def send(i, carry):
            other = lax.rem(me + i, n_ep)
            pltpu.make_async_remote_copy(
                src_ref=source.at[other],
                dst_ref=target.at[me],
                send_sem=sems.at[0],
                recv_sem=sems.at[1],
                device_id={"ep": other},
                device_id_type=MESH,
            ).start()
            return carry

        lax.fori_loop(1, n_ep, send, 0)
        own = pltpu.make_async_copy(source.at[me], target.at[me], sems.at[2])
        own.start()

        def received():
            own.wait()
            rest = target.at[pl.ds(0, n_ep - 1)]
            pltpu.make_async_copy(rest, rest, sems.at[1]).wait()

        def sent():
            rest = source.at[pl.ds(0, n_ep - 1)]
            pltpu.make_async_copy(rest, rest, sems.at[0]).wait()

        return received, sent

    order = (0, 3, 1, 2)
    out_waits = []
    for i, off in enumerate(order):
        if i > 0:
            scaled_copies[n_kv - off - 1].wait()
        if i == n_kv - 1:
            pump(range(3, 6), range(3, items), range(1, 3))
        quarter = scaled_all[lax.rem(q + off, n_kv)]
        normed = (quarter.astype(jnp.float32) * inv_first).astype(jnp.bfloat16)
        picked = dot(pick_t[...], normed).reshape(experts, share, cols)
        sends[i] = picked.astype(jnp.bfloat16)
        out_waits.append(all_to_all(sends.at[i], arrived.at[i], out_sem.at[i]))

    second_on(0)
    for t in range(3, wide_items):
        pump(range(t + 3, t + 4), (), range(t, t + 1))
        second_on(t - 2)
    pump(range(wide_items + 3, items), (), range(wide_items, wide_items + 2))
    for t in range(wide_items - 2, wide_items):
        second_on(t)
    pump((), (), range(wide_items + 2, items))
    logits_t = stats[0:experts, :] * inv_t
    totals = jnp.sum(jnp.where(naming(device_of) > 0, jnp.exp(logits_t), 0.0), axis=0, keepdims=True)
    turned = jnp.where(side == 0, pltpu.roll(logits_t, 1, 0), pltpu.roll(logits_t, experts - 1, 0))
    served = jnp.where(device_of % 2 == side, logits_t, turned)
    gate_t = jnp.where(code_t[...] >= 0, jnp.exp(served), 0.0) / totals
    mix_high, mix_low = split_two(
        (
            jnp.broadcast_to(gate_t[:, None, :], (experts, share, rows))
            .reshape(experts * share, rows)
            * pick_t[...].astype(jnp.float32)
        ).T
    )
    for received, _ in out_waits:
        received()

    tile_blocks = 32
    tile_rows = tile_blocks * share

    def expert_in(c):
        def tile(m, carry):
            block = pl.multiple_of(m * tile_blocks, tile_blocks)
            row = pl.multiple_of(m * tile_rows, tile_rows)
            g = jnp.zeros((tile_rows, gates.shape[2]), jnp.float32)
            u = jnp.zeros((tile_rows, gates.shape[2]), jnp.float32)
            for i, off in enumerate(order):
                x = arrived[i, pl.ds(block, tile_blocks)].reshape(tile_rows, cols)
                some = pl.ds(pl.multiple_of(lax.rem(q + off, n_kv) * cols, cols), cols)
                g = g + dot(x, gates[c, some, :])
                u = u + dot(x, ups[c, some, :])
            acts[c, pl.ds(row, tile_rows), :] = (g / (1.0 + jnp.exp(-g)) * u).astype(jnp.bfloat16)
            return carry

        lax.fori_loop(0, n_ep // tile_blocks, tile, 0)

    def expert_out(n):
        span = pl.ds(n * cols, cols)

        def tile(m, carry):
            block = pl.multiple_of(m * tile_blocks, tile_blocks)
            row = pl.multiple_of(m * tile_rows, tile_rows)
            term = jnp.zeros((tile_rows, cols), jnp.float32)
            for c in range(n_kv):
                term = term + dot(acts[c, pl.ds(row, tile_rows), :], downs[c, :, span])
            replies[n, pl.ds(block, tile_blocks)] = term.reshape(
                tile_blocks, share, cols
            ).astype(jnp.bfloat16)
            return carry

        lax.fori_loop(0, n_ep // tile_blocks, tile, 0)

    for c in range(2):
        expert_in(c)
    for kind in range(2, 4):
        for t in range(wide_items):
            move(kind, t).wait_recv()
        expert_in(kind)
    second_on(wide_items)
    back_waits = []
    for n in range(n_kv):
        if n + 1 < n_kv:
            second_on(wide_items + n + 1)
        for kind in range(2, 4):
            move(kind, wide_items + n).wait_recv()
        expert_out(n)
        back_waits.append(all_to_all(replies.at[n], returned.at[n], back_sem.at[n]))
    for _, sent in out_waits:
        sent()
    for t in range(items):
        for kind in range(1, 4):
            move(kind, t).wait_send()

    @pl.when(jnp.logical_not(home))
    def _():
        for t in range(items):
            move(0, t).wait_send()

    def part_copy(n):
        place = lax.rem(q - n + n_kv, n_kv) - 1
        return pltpu.make_async_remote_copy(
            src_ref=part_out.at[n],
            dst_ref=part_in.at[place],
            send_sem=part_sem.at[0, n],
            recv_sem=part_sem.at[1, place],
            device_id={"kv": n},
            device_id_type=MESH,
        )

    for n in range(n_kv):
        back_waits[n][0]()
        back = returned[n].reshape(experts * share, cols)
        part_out[n] = (dot(mix_high, back) + dot(mix_low, back)).astype(jnp.bfloat16)

        @pl.when(q != n)
        def _():
            part_copy(n).start()

    combined = hidden[...] + part_out[q].astype(jnp.float32)
    for d in range(1, n_kv):
        pltpu.make_async_copy(part_in.at[d - 1], part_in.at[d - 1], part_sem.at[1, d - 1]).wait()
        combined = combined + part_in[d - 1].astype(jnp.float32)
    own_square = jnp.sum(combined * combined, axis=1, keepdims=True)
    square_all[q] = jnp.broadcast_to(own_square, (rows, 128)).T[0:8, :]
    square_copies = exchange(square_all, square_sem)
    for _, sent in back_waits:
        sent()
    for n in range(n_kv):

        @pl.when(q != n)
        def _():
            part_copy(n).wait_send()

    for copy in square_copies:
        copy.wait()
    square = square_all[0]
    for j in range(1, n_kv):
        square = square + square_all[j]
    inv_row = lax.rsqrt(square[0:1] / width + epsilon)
    inv_second = jnp.broadcast_to(inv_row, (128, rows)).T[:, 0:1]
    out[...] = (combined * inv_second * final_gain[...]).astype(out.dtype)


def make_per_device(n_ep, n_kv):
    def per_device(
        queries,
        key_pool,
        value_pool,
        page_table,
        lengths,
        prefill_attn,
        residual,
        w_out,
        norm_gain,
        router,
        w_gate,
        w_up,
        w_down,
        final_gain,
        routes,
    ):
        width = queries.shape[1]
        rows, cols = residual.shape
        experts = router.shape[1]
        share = min(rows, 2 * rows * TOP // experts) // n_kv
        tokens = key_pool.shape[0] * key_pool.shape[1]
        packed = 3 * queries.shape[0]
        f32, bf16 = jnp.float32, jnp.bfloat16
        vmem = pl.BlockSpec(memory_space=pltpu.VMEM)
        smem = pl.BlockSpec(memory_space=pltpu.SMEM)
        anywhere = pl.BlockSpec(memory_space=pl.ANY)
        dma = pltpu.SemaphoreType.DMA
        return pl.pallas_call(
            lambda *refs: layer_kernel(n_ep, n_kv, *refs),
            name="layer",
            out_shape=jax.ShapeDtypeStruct((rows, cols), bf16),
            in_specs=[vmem, anywhere, anywhere, smem, smem, vmem, vmem, anywhere, vmem, vmem]
            + [anywhere] * 3
            + [vmem, vmem],
            out_specs=vmem,
            scratch_shapes=[
                pltpu.VMEM((tokens, width), bf16),
                pltpu.VMEM((tokens, width), bf16),
                pltpu.VMEM(w_out.shape, bf16),
                pltpu.VMEM((rows, width), bf16),
                pltpu.VMEM((n_kv, packed, width), f32),
                pltpu.VMEM((n_kv, experts + 8, rows), f32),
                pltpu.VMEM((n_kv, rows, cols), bf16),
                pltpu.VMEM((rows, cols), f32),
                pltpu.VMEM((experts, rows), jnp.int32),
                pltpu.VMEM((experts * share, rows), bf16),
                pltpu.VMEM((n_kv, experts, share, cols), bf16),
                pltpu.VMEM((n_kv, experts, share, cols), bf16),
                pltpu.VMEM((n_kv,) + w_gate.shape[1:], bf16),
                pltpu.VMEM((n_kv,) + w_up.shape[1:], bf16),
                pltpu.VMEM((n_kv,) + w_down.shape[1:], bf16),
                pltpu.VMEM((n_kv, experts * share, w_gate.shape[2]), bf16),
                pltpu.VMEM((n_kv, experts, share, cols), bf16),
                pltpu.VMEM((n_kv, experts, share, cols), bf16),
                pltpu.VMEM((n_kv, rows, cols), bf16),
                pltpu.VMEM((n_kv - 1, rows, cols), bf16),
                pltpu.VMEM((n_kv, 8, rows), f32),
                dma((6,)),
                dma((2, n_kv - 1)),
                dma((2, n_kv - 1)),
                dma((2, n_kv - 1)),
                dma((2, 4, 12)),
                dma((n_kv, 3)),
                dma((n_kv, 3)),
                dma((2, n_kv)),
                dma((2, n_kv - 1)),
            ],
            compiler_params=pltpu.CompilerParams(
                collective_id=0, has_side_effects=True, vmem_limit_bytes=60 << 20
            ),
        )(
            queries,
            key_pool.reshape(tokens, width),
            value_pool.reshape(tokens, width),
            page_table,
            lengths,
            prefill_attn,
            residual,
            w_out,
            norm_gain.reshape(1, cols),
            router.T,
            w_gate,
            w_up,
            w_down,
            final_gain.reshape(1, cols),
            routes.T,
        )

    return per_device


def solution(mesh):
    placed = (
        P("ep", None),
        P(("ep", "kv"), None, None),
        P(("ep", "kv"), None, None),
        P("ep", "kv", None),
        P("ep"),
        P("ep", None),
        P("ep", "kv"),
        P(None, "kv"),
        P("kv"),
        P("kv", None),
        P("ep", None, "kv"),
        P("ep", None, "kv"),
        P("ep", "kv", None),
        P("kv"),
        P("ep", None),
    )
    return jax.shard_map(
        make_per_device(mesh.shape["ep"], mesh.shape["kv"]),
        mesh=mesh,
        in_specs=placed,
        out_specs=P("ep", "kv"),
        check_vma=False,
    )
```

```python
import math

import jax
import jax.numpy as jnp
from jax import lax
from jax.experimental import pallas as pl
from jax.experimental.pallas import tpu as pltpu
from jax.sharding import PartitionSpec as P

HEAD_DIM = 128
TOP = 8

epsilon = 1e-06
floor_score = -1e30
MESH = pl.DeviceIdType.MESH


def split_two(v):
    high = v.astype(jnp.bfloat16)
    low = (v - high.astype(jnp.float32)).astype(jnp.bfloat16)
    return high, low


def iota(shape, axis):
    return lax.broadcasted_iota(jnp.int32, shape, axis)


def dot(a, b):
    return jnp.dot(a, b, preferred_element_type=jnp.float32)


def layer_kernel(
    n_ep,
    n_kv,
    queries,
    key_pool,
    value_pool,
    page_table,
    lengths,
    prefill,
    residual,
    w_out,
    norm_gain,
    router_t,
    w_gate,
    w_up,
    w_down,
    final_gain,
    routes_t,
    out,
    kbuf,
    vbuf,
    wobuf,
    attn,
    pack_all,
    stat_all,
    scaled_all,
    hidden,
    code_t,
    pick_t,
    sends,
    arrived,
    gates,
    ups,
    downs,
    inv_out,
    inv_in,
    inv_wide,
    total,
    acts,
    replies,
    returned,
    part_out,
    part_in,
    square_all,
    load_sem,
    pack_sem,
    stat_sem,
    scaled_sem,
    ring_sem,
    inv_sem,
    out_sem,
    back_sem,
    part_sem,
    square_sem,
):
    me = lax.axis_index("ep")
    q = lax.axis_index("kv")
    rows, cols = hidden.shape
    width = cols * n_kv
    requests = queries.shape[0]
    heads = width // HEAD_DIM
    experts, share = sends.shape[1], sends.shape[2]
    tokens = kbuf.shape[0]
    page_rows = tokens // (requests * page_table.shape[2])

    def peer(d):
        return {"kv": lax.rem(q + d, n_kv)}

    side = q // 2
    core = lax.rem(me, 2)
    home = core == side
    sibling = {"ep": me + 1 - 2 * core}
    partner = {"kv": q + 1 - 2 * lax.rem(q, 2)}
    across = {"kv": n_kv - 1 - q, "ep": me + 1 - 2 * core}

    loads = [
        pltpu.make_async_copy(key_pool, kbuf, load_sem.at[0]),
        pltpu.make_async_copy(value_pool, vbuf, load_sem.at[1]),
        pltpu.make_async_copy(w_out, wobuf, load_sem.at[2]),
    ]
    for load in loads:
        load.start()
    own_loads = [
        pltpu.make_async_copy(w_gate.at[0], gates.at[0], load_sem.at[3]),
        pltpu.make_async_copy(w_up.at[0], ups.at[0], load_sem.at[4]),
        pltpu.make_async_copy(w_down.at[0], downs.at[0], load_sem.at[5]),
    ]

    @pl.when(home)
    def _():
        for load in own_loads:
            load.start()

    barrier = pltpu.get_barrier_semaphore()

    def greet(i, carry):
        pl.semaphore_signal(
            barrier, inc=1, device_id={"ep": lax.rem(me + i, n_ep)}, device_id_type=MESH
        )
        return carry

    lax.fori_loop(1, n_ep, greet, 0)
    for d in range(1, n_kv):
        pl.semaphore_signal(barrier, inc=1, device_id=peer(d), device_id_type=MESH)
    pl.semaphore_signal(barrier, inc=1, device_id=across, device_id_type=MESH)

    on_head = iota((heads, width), 1) // HEAD_DIM == iota((heads, width), 0)
    spread = jnp.concatenate(
        [
            jnp.where(on_head, queries[r : r + 1, :].astype(jnp.float32), 0.0)
            for r in range(requests)
        ],
        axis=0,
    ).astype(jnp.bfloat16)
    lane = iota((heads, tokens), 1)
    page_of, in_page = lane // page_rows, lane % page_rows
    seen = []
    for r in range(requests):
        place = jnp.full((heads, tokens), 1 << 30, jnp.int32)
        for j in range(page_table.shape[2]):
            first = (j * n_kv + q) * page_rows
            place = jnp.where(page_of == page_table[r, 0, j], first + in_page, place)
        seen.append((place < lengths[r]).astype(jnp.int32))
    visible = jnp.concatenate(seen, axis=0) > 0
    loads[0].wait()
    scores = lax.dot_general(
        spread, kbuf[...], (((1,), (1,)), ((), ())), preferred_element_type=jnp.float32
    ) * (1.0 / math.sqrt(HEAD_DIM))
    masked = jnp.where(visible, scores, floor_score)
    peak = jnp.max(masked, axis=1, keepdims=True)
    weights = jnp.where(visible, jnp.exp(masked - peak), 0.0)
    mass = jnp.sum(weights, axis=1, keepdims=True)
    high, low = split_two(weights)
    loads[1].wait()
    wide = dot(high, vbuf[...]) + dot(low, vbuf[...])

    def on_lanes(values, r):
        part = jnp.broadcast_to(values[r * heads : (r + 1) * heads], (heads, width))
        return jnp.sum(jnp.where(on_head, part, 0.0), axis=0, keepdims=True)

    for r in range(requests):
        for i, item in enumerate((wide, peak, mass)):
            pack_all[q, i * requests + r : i * requests + r + 1, :] = on_lanes(item, r)

    pl.semaphore_wait(barrier, n_ep - 1 + n_kv)

    def exchange(ref, sems):
        copies = []
        for d in range(1, n_kv):
            copies.append(
                pltpu.make_async_remote_copy(
                    src_ref=ref.at[q],
                    dst_ref=ref.at[q],
                    send_sem=sems.at[0, d - 1],
                    recv_sem=sems.at[1, d - 1],
                    device_id=peer(d),
                    device_id_type=MESH,
                )
            )
            copies[-1].start()
        return copies

    pack_copies = exchange(pack_all, pack_sem)

    piece = gates.shape[1] // 4
    wide_items, items = 8, 12

    def view(slot, t):
        if t < wide_items:
            return (gates, ups)[t // 4].at[slot, pl.ds(t % 4 * piece, piece)]
        return downs.at[slot, :, pl.ds((t - wide_items) * cols, cols)]

    def own_view(t):
        if t < wide_items:
            return (w_gate, w_up)[t // 4].at[0, pl.ds(t % 4 * piece, piece)]
        return w_down.at[0, :, pl.ds((t - wide_items) * cols, cols)]

    def move(kind, t):
        source, slot, device = (
            (own_view(t), 0, across),
            (view(0, t), 1, partner),
            (view(0, t), 2, sibling),
            (view(1, t), 3, sibling),
        )[kind]
        return pltpu.make_async_remote_copy(
            src_ref=source,
            dst_ref=view(slot, t),
            send_sem=ring_sem.at[0, kind, t],
            recv_sem=ring_sem.at[1, kind, t],
            device_id=device,
            device_id_type=MESH,
        )

    def first_on(t):
        move(1, t).start()
        move(2, t).start()

    def second_on(t):
        move(1, t).wait_recv()
        move(3, t).start()

    def pump(home_items, cross_items, guest_items):
        @pl.when(home)
        def _():
            for t in home_items:
                first_on(t)

        @pl.when(jnp.logical_not(home))
        def _():
            for t in cross_items:
                move(0, t).start()
            for t in guest_items:
                move(0, t).wait_recv()
                first_on(t)

    @pl.when(home)
    def _():
        for load in own_loads:
            load.wait()

    pump(range(0, 1), range(0, 2), ())

    def naming(expert_of):
        named = jnp.zeros((experts, rows), jnp.float32)
        for k in range(TOP):
            named = jnp.where(expert_of == routes_t[k : k + 1, :], 1.0, named)
        return named

    device_of = iota((experts, rows), 0)
    named = naming(device_of // 2 * 2 + side)
    before = (iota((rows, rows), 0) < iota((rows, rows), 1)).astype(jnp.float32)
    rank = dot(named.astype(jnp.bfloat16), before.astype(jnp.bfloat16))
    code_t[...] = jnp.where(named > 0, rank, -1.0).astype(jnp.int32)
    slot = (lax.rem(q, 2) * 2 + iota((experts, share, rows), 0) % 2) * share + iota(
        (experts, share, rows), 1
    )
    pick = (code_t[...][:, None, :] == slot).astype(jnp.float32).reshape(experts * share, rows)
    pick_t[...] = pick.astype(jnp.bfloat16)

    loads[2].wait()
    attn[0 : prefill.shape[0], :] = prefill[...]
    for copy in pack_copies:
        copy.wait()
    packs = pack_all[...]
    sums = packs[:, 0:requests]
    peaks = packs[:, requests : 2 * requests]
    masses = packs[:, 2 * requests : 3 * requests]
    factors = jnp.exp(peaks - jnp.max(peaks, axis=0)[None])
    attn[prefill.shape[0] :, :] = (
        jnp.sum(sums * factors, axis=0) / jnp.sum(masses * factors, axis=0)
    ).astype(jnp.bfloat16)
    state = residual[...].astype(jnp.float32) + dot(attn[...], wobuf[...])
    hidden[...] = state
    scaled = (state * norm_gain[...]).astype(jnp.bfloat16)
    scaled_all[q] = scaled
    squares = jnp.sum(state * state, axis=1, keepdims=True)
    scores_of = lax.dot_general(
        scaled, router_t[...], (((1,), (1,)), ((), ())), preferred_element_type=jnp.float32
    )
    stat = jnp.concatenate([scores_of, jnp.broadcast_to(squares, (rows, 128 - experts))], axis=1)
    stat_all[q] = stat.T[0 : stat_all.shape[1], :]
    stat_copies = exchange(stat_all, stat_sem)
    scaled_copies = exchange(scaled_all, scaled_sem)
    pump(range(1, 3), range(2, 3), range(0, 1))
    def all_to_all(source, target, sems):
        def send(i, carry):
            other = lax.rem(me + i, n_ep)
            pltpu.make_async_remote_copy(
                src_ref=source.at[other],
                dst_ref=target.at[me],
                send_sem=sems.at[0],
                recv_sem=sems.at[1],
                device_id={"ep": other},
                device_id_type=MESH,
            ).start()
            return carry

        lax.fori_loop(1, n_ep, send, 0)
        own = pltpu.make_async_copy(source.at[me], target.at[me], sems.at[2])
        own.start()

        def received():
            own.wait()
            rest = target.at[pl.ds(0, n_ep - 1)]
            pltpu.make_async_copy(rest, rest, sems.at[1]).wait()

        def sent():
            rest = source.at[pl.ds(0, n_ep - 1)]
            pltpu.make_async_copy(rest, rest, sems.at[0]).wait()

        return received, sent

    order = (0, 3, 1, 2)
    out_waits = []

    def dispatch(i):
        picked = dot(pick_t[...], scaled_all[lax.rem(q + order[i], n_kv)])
        sends[i] = picked.reshape(experts, share, cols).astype(jnp.bfloat16)
        out_waits.append(all_to_all(sends.at[i], arrived.at[i], out_sem.at[i]))

    dispatch(0)
    for copy in stat_copies:
        copy.wait()
    stats = stat_all[0]
    for j in range(1, n_kv):
        stats = stats + stat_all[j]
    inv_t = lax.rsqrt(stats[experts : experts + 1, :] / width + epsilon)
    for copy in scaled_copies:
        copy.wait()
    pump(range(3, 6), range(3, items), range(1, 3))
    for i in range(1, n_kv - 1):
        dispatch(i)
    on_lane = iota((experts, share, rows), 2) == iota((experts, share, rows), 1)
    slot_pick = pick_t[...].astype(jnp.float32).reshape(experts, share, rows)
    slot_inv = jnp.sum(slot_pick * inv_t[None], axis=2, keepdims=True)
    inv_out[...] = jnp.sum(jnp.where(on_lane, slot_inv, 0.0), axis=1, keepdims=True)
    inv_received, inv_sent = all_to_all(inv_out, inv_in, inv_sem)
    dispatch(n_kv - 1)
    second_on(0)
    for t in range(3, wide_items):
        pump(range(t + 3, t + 4), (), range(t, t + 1))
        second_on(t - 2)
    pump(range(wide_items + 3, items), (), range(wide_items, wide_items + 2))
    for t in range(wide_items - 2, wide_items):
        second_on(t)
    pump((), (), range(wide_items + 2, items))
    logits_t = stats[0:experts, :] * inv_t
    totals = jnp.sum(jnp.where(naming(device_of) > 0, jnp.exp(logits_t), 0.0), axis=0, keepdims=True)
    turned = jnp.where(side == 0, pltpu.roll(logits_t, 1, 0), pltpu.roll(logits_t, experts - 1, 0))
    served = jnp.where(device_of % 2 == side, logits_t, turned)
    gate_t = jnp.where(code_t[...] >= 0, jnp.exp(served), 0.0) / totals
    mix_high, mix_low = split_two(
        (
            jnp.broadcast_to(gate_t[:, None, :], (experts, share, rows))
            .reshape(experts * share, rows)
            * pick_t[...].astype(jnp.float32)
        ).T
    )
    tile_blocks = 32
    tile_rows = tile_blocks * share

    hidden_cols = gates.shape[2]

    def expert_in(c, first, last):
        def tile(m, carry):
            block = pl.multiple_of(m * tile_blocks, tile_blocks)
            row = pl.multiple_of(m * tile_rows, tile_rows)
            if first == 0:
                g = jnp.zeros((tile_rows, hidden_cols), jnp.float32)
                u = jnp.zeros((tile_rows, hidden_cols), jnp.float32)
            else:
                g = total[c, 0, pl.ds(row, tile_rows), :]
                u = total[c, 1, pl.ds(row, tile_rows), :]
            for i in range(first, last):
                off = order[i]
                x = arrived[i, pl.ds(block, tile_blocks)].reshape(tile_rows, cols)
                some = pl.ds(pl.multiple_of(lax.rem(q + off, n_kv) * cols, cols), cols)
                g = g + dot(x, gates[c, some, :])
                u = u + dot(x, ups[c, some, :])
            if last < n_kv:
                total[c, 0, pl.ds(row, tile_rows), :] = g
                total[c, 1, pl.ds(row, tile_rows), :] = u
            else:
                g = g * inv_wide[pl.ds(row, tile_rows), :]
                u = u * inv_wide[pl.ds(row, tile_rows), :]
                act = (g / (1.0 + jnp.exp(-g)) * u).astype(jnp.bfloat16)
                acts[c, pl.ds(row, tile_rows), :] = act
            return carry

        lax.fori_loop(0, n_ep // tile_blocks, tile, 0)

    def expert_out(n):
        span = pl.ds(n * cols, cols)

        def tile(m, carry):
            block = pl.multiple_of(m * tile_blocks, tile_blocks)
            row = pl.multiple_of(m * tile_rows, tile_rows)
            term = jnp.zeros((tile_rows, cols), jnp.float32)
            for c in range(n_kv):
                term = term + dot(acts[c, pl.ds(row, tile_rows), :], downs[c, :, span])
            replies[n, pl.ds(block, tile_blocks)] = term.reshape(
                tile_blocks, share, cols
            ).astype(jnp.bfloat16)
            return carry

        lax.fori_loop(0, n_ep // tile_blocks, tile, 0)

    for i in range(n_kv - 1):
        out_waits[i][0]()
    for c in range(n_kv):
        if c >= 2:
            for t in range(wide_items):
                move(c, t).wait_recv()
        expert_in(c, 0, n_kv - 1)
    inv_received()
    slot_inv = jnp.sum(
        jnp.where(on_lane, jnp.broadcast_to(inv_in[...], (experts, share, rows)), 0.0),
        axis=2,
        keepdims=True,
    ).reshape(experts * share, 1)
    inv_wide[...] = jnp.broadcast_to(slot_inv, inv_wide.shape)
    out_waits[n_kv - 1][0]()
    for c in range(n_kv):
        expert_in(c, n_kv - 1, n_kv)
    second_on(wide_items)
    back_waits = []
    for n in range(n_kv):
        if n + 1 < n_kv:
            second_on(wide_items + n + 1)
        for kind in range(2, 4):
            move(kind, wide_items + n).wait_recv()
        expert_out(n)
        back_waits.append(all_to_all(replies.at[n], returned.at[n], back_sem.at[n]))
    for _, sent in out_waits:
        sent()
    inv_sent()
    for t in range(items):
        for kind in range(1, 4):
            move(kind, t).wait_send()

    @pl.when(jnp.logical_not(home))
    def _():
        for t in range(items):
            move(0, t).wait_send()

    def part_copy(n):
        place = lax.rem(q - n + n_kv, n_kv) - 1
        return pltpu.make_async_remote_copy(
            src_ref=part_out.at[n],
            dst_ref=part_in.at[place],
            send_sem=part_sem.at[0, n],
            recv_sem=part_sem.at[1, place],
            device_id={"kv": n},
            device_id_type=MESH,
        )

    for n in range(n_kv):
        back_waits[n][0]()
        back = returned[n].reshape(experts * share, cols)
        part_out[n] = (dot(mix_high, back) + dot(mix_low, back)).astype(jnp.bfloat16)

        @pl.when(q != n)
        def _():
            part_copy(n).start()

    combined = hidden[...] + part_out[q].astype(jnp.float32)
    for d in range(1, n_kv):
        pltpu.make_async_copy(part_in.at[d - 1], part_in.at[d - 1], part_sem.at[1, d - 1]).wait()
        combined = combined + part_in[d - 1].astype(jnp.float32)
    own_square = jnp.sum(combined * combined, axis=1, keepdims=True)
    square_all[q] = jnp.broadcast_to(own_square, (rows, 128)).T[0:8, :]
    square_copies = exchange(square_all, square_sem)
    for _, sent in back_waits:
        sent()
    for n in range(n_kv):

        @pl.when(q != n)
        def _():
            part_copy(n).wait_send()

    for copy in square_copies:
        copy.wait()
    square = square_all[0]
    for j in range(1, n_kv):
        square = square + square_all[j]
    inv_row = lax.rsqrt(square[0:1] / width + epsilon)
    inv_second = jnp.broadcast_to(inv_row, (128, rows)).T[:, 0:1]
    out[...] = (combined * inv_second * final_gain[...]).astype(out.dtype)


def make_per_device(n_ep, n_kv):
    def per_device(
        queries,
        key_pool,
        value_pool,
        page_table,
        lengths,
        prefill_attn,
        residual,
        w_out,
        norm_gain,
        router,
        w_gate,
        w_up,
        w_down,
        final_gain,
        routes,
    ):
        width = queries.shape[1]
        rows, cols = residual.shape
        experts = router.shape[1]
        share = min(rows, 2 * rows * TOP // experts) // n_kv
        tokens = key_pool.shape[0] * key_pool.shape[1]
        packed = 3 * queries.shape[0]
        f32, bf16 = jnp.float32, jnp.bfloat16
        vmem = pl.BlockSpec(memory_space=pltpu.VMEM)
        smem = pl.BlockSpec(memory_space=pltpu.SMEM)
        anywhere = pl.BlockSpec(memory_space=pl.ANY)
        dma = pltpu.SemaphoreType.DMA
        return pl.pallas_call(
            lambda *refs: layer_kernel(n_ep, n_kv, *refs),
            name="layer",
            out_shape=jax.ShapeDtypeStruct((rows, cols), bf16),
            in_specs=[vmem, anywhere, anywhere, smem, smem, vmem, vmem, anywhere, vmem, vmem]
            + [anywhere] * 3
            + [vmem, vmem],
            out_specs=vmem,
            scratch_shapes=[
                pltpu.VMEM((tokens, width), bf16),
                pltpu.VMEM((tokens, width), bf16),
                pltpu.VMEM(w_out.shape, bf16),
                pltpu.VMEM((rows, width), bf16),
                pltpu.VMEM((n_kv, packed, width), f32),
                pltpu.VMEM((n_kv, experts + 8, rows), f32),
                pltpu.VMEM((n_kv, rows, cols), bf16),
                pltpu.VMEM((rows, cols), f32),
                pltpu.VMEM((experts, rows), jnp.int32),
                pltpu.VMEM((experts * share, rows), bf16),
                pltpu.VMEM((n_kv, experts, share, cols), bf16),
                pltpu.VMEM((n_kv, experts, share, cols), bf16),
                pltpu.VMEM((n_kv,) + w_gate.shape[1:], bf16),
                pltpu.VMEM((n_kv,) + w_up.shape[1:], bf16),
                pltpu.VMEM((n_kv,) + w_down.shape[1:], bf16),
                pltpu.VMEM((experts, 1, rows), f32),
                pltpu.VMEM((experts, 1, rows), f32),
                pltpu.VMEM((experts * share, w_gate.shape[2]), f32),
                pltpu.VMEM((n_kv, 2, experts * share, w_gate.shape[2]), f32),
                pltpu.VMEM((n_kv, experts * share, w_gate.shape[2]), bf16),
                pltpu.VMEM((n_kv, experts, share, cols), bf16),
                pltpu.VMEM((n_kv, experts, share, cols), bf16),
                pltpu.VMEM((n_kv, rows, cols), bf16),
                pltpu.VMEM((n_kv - 1, rows, cols), bf16),
                pltpu.VMEM((n_kv, 8, rows), f32),
                dma((6,)),
                dma((2, n_kv - 1)),
                dma((2, n_kv - 1)),
                dma((2, n_kv - 1)),
                dma((2, 4, 12)),
                dma((3,)),
                dma((n_kv, 3)),
                dma((n_kv, 3)),
                dma((2, n_kv)),
                dma((2, n_kv - 1)),
            ],
            compiler_params=pltpu.CompilerParams(
                collective_id=0, has_side_effects=True, vmem_limit_bytes=60 << 20
            ),
        )(
            queries,
            key_pool.reshape(tokens, width),
            value_pool.reshape(tokens, width),
            page_table,
            lengths,
            prefill_attn,
            residual,
            w_out,
            norm_gain.reshape(1, cols),
            router.T,
            w_gate,
            w_up,
            w_down,
            final_gain.reshape(1, cols),
            routes.T,
        )

    return per_device


def solution(mesh):
    placed = (
        P("ep", None),
        P(("ep", "kv"), None, None),
        P(("ep", "kv"), None, None),
        P("ep", "kv", None),
        P("ep"),
        P("ep", None),
        P("ep", "kv"),
        P(None, "kv"),
        P("kv"),
        P("kv", None),
        P("ep", None, "kv"),
        P("ep", None, "kv"),
        P("ep", "kv", None),
        P("kv"),
        P("ep", None),
    )
    return jax.shard_map(
        make_per_device(mesh.shape["ep"], mesh.shape["kv"]),
        mesh=mesh,
        in_specs=placed,
        out_specs=P("ep", "kv"),
        check_vma=False,
    )
```

```python
import math

import jax
import jax.numpy as jnp
from jax import lax
from jax.experimental import pallas as pl
from jax.experimental.pallas import tpu as pltpu
from jax.sharding import PartitionSpec as P

HEAD_DIM = 128
TOP = 8

epsilon = 1e-06
floor_score = -1e30
MESH = pl.DeviceIdType.MESH


def split_two(v):
    high = v.astype(jnp.bfloat16)
    low = (v - high.astype(jnp.float32)).astype(jnp.bfloat16)
    return high, low


def iota(shape, axis):
    return lax.broadcasted_iota(jnp.int32, shape, axis)


def dot(a, b):
    return jnp.dot(a, b, preferred_element_type=jnp.float32)


def layer_kernel(
    n_ep,
    n_kv,
    queries,
    key_pool,
    value_pool,
    page_table,
    lengths,
    prefill,
    residual,
    w_out,
    norm_gain,
    router_t,
    w_gate,
    w_up,
    w_down,
    final_gain,
    routes_t,
    out,
    kbuf,
    vbuf,
    wobuf,
    attn,
    pack_all,
    stat_all,
    scaled_all,
    hidden,
    code_t,
    pick_t,
    sends,
    arrived,
    gates,
    ups,
    downs,
    inv_out,
    inv_in,
    inv_wide,
    total,
    acts,
    replies,
    returned,
    part_out,
    part_in,
    square_all,
    load_sem,
    pack_sem,
    stat_sem,
    scaled_sem,
    ring_sem,
    inv_sem,
    out_sem,
    back_sem,
    part_sem,
    square_sem,
):
    me = lax.axis_index("ep")
    q = lax.axis_index("kv")
    rows, cols = hidden.shape
    width = cols * n_kv
    requests = queries.shape[0]
    heads = width // HEAD_DIM
    experts, share = sends.shape[1], sends.shape[2]
    tokens = kbuf.shape[0]
    page_rows = tokens // (requests * page_table.shape[2])

    def peer(d):
        return {"kv": lax.rem(q + d, n_kv)}

    side = q // 2
    core = lax.rem(me, 2)
    home = core == side
    sibling = {"ep": me + 1 - 2 * core}
    partner = {"kv": q + 1 - 2 * lax.rem(q, 2)}
    across = {"kv": n_kv - 1 - q, "ep": me + 1 - 2 * core}

    loads = [
        pltpu.make_async_copy(key_pool, kbuf, load_sem.at[0]),
        pltpu.make_async_copy(value_pool, vbuf, load_sem.at[1]),
        pltpu.make_async_copy(w_out, wobuf, load_sem.at[2]),
    ]
    for load in loads:
        load.start()
    own_loads = [
        pltpu.make_async_copy(w_gate.at[0], gates.at[0], load_sem.at[3]),
        pltpu.make_async_copy(w_up.at[0], ups.at[0], load_sem.at[4]),
        pltpu.make_async_copy(w_down.at[0], downs.at[0], load_sem.at[5]),
    ]

    @pl.when(home)
    def _():
        for load in own_loads:
            load.start()

    barrier = pltpu.get_barrier_semaphore()

    def greet(i, carry):
        pl.semaphore_signal(
            barrier, inc=1, device_id={"ep": lax.rem(me + i, n_ep)}, device_id_type=MESH
        )
        return carry

    lax.fori_loop(1, n_ep, greet, 0)
    for d in range(1, n_kv):
        pl.semaphore_signal(barrier, inc=1, device_id=peer(d), device_id_type=MESH)
    pl.semaphore_signal(barrier, inc=1, device_id=across, device_id_type=MESH)

    on_head = iota((heads, width), 1) // HEAD_DIM == iota((heads, width), 0)
    spread = jnp.concatenate(
        [
            jnp.where(on_head, queries[r : r + 1, :].astype(jnp.float32), 0.0)
            for r in range(requests)
        ],
        axis=0,
    ).astype(jnp.bfloat16)
    lane = iota((heads, tokens), 1)
    page_of, in_page = lane // page_rows, lane % page_rows
    seen = []
    for r in range(requests):
        place = jnp.full((heads, tokens), 1 << 30, jnp.int32)
        for j in range(page_table.shape[2]):
            first = (j * n_kv + q) * page_rows
            place = jnp.where(page_of == page_table[r, 0, j], first + in_page, place)
        seen.append((place < lengths[r]).astype(jnp.int32))
    visible = jnp.concatenate(seen, axis=0) > 0
    loads[0].wait()
    scores = lax.dot_general(
        spread, kbuf[...], (((1,), (1,)), ((), ())), preferred_element_type=jnp.float32
    ) * (1.0 / math.sqrt(HEAD_DIM))
    masked = jnp.where(visible, scores, floor_score)
    peak = jnp.max(masked, axis=1, keepdims=True)
    weights = jnp.where(visible, jnp.exp(masked - peak), 0.0)
    mass = jnp.sum(weights, axis=1, keepdims=True)
    high, low = split_two(weights)
    loads[1].wait()
    wide = dot(high, vbuf[...]) + dot(low, vbuf[...])

    def on_lanes(values, r):
        part = jnp.broadcast_to(values[r * heads : (r + 1) * heads], (heads, width))
        return jnp.sum(jnp.where(on_head, part, 0.0), axis=0, keepdims=True)

    for r in range(requests):
        for i, item in enumerate((wide, peak, mass)):
            pack_all[q, i * requests + r : i * requests + r + 1, :] = on_lanes(item, r)

    pl.semaphore_wait(barrier, n_ep - 1 + n_kv)

    def exchange(ref, sems):
        copies = []
        for d in range(1, n_kv):
            copies.append(
                pltpu.make_async_remote_copy(
                    src_ref=ref.at[q],
                    dst_ref=ref.at[q],
                    send_sem=sems.at[0, d - 1],
                    recv_sem=sems.at[1, d - 1],
                    device_id=peer(d),
                    device_id_type=MESH,
                )
            )
            copies[-1].start()
        return copies

    pack_copies = exchange(pack_all, pack_sem)

    piece = gates.shape[1] // 4
    wide_items, items = 8, 12

    def view(slot, t):
        if t < wide_items:
            return (gates, ups)[t // 4].at[slot, pl.ds(t % 4 * piece, piece)]
        return downs.at[slot, :, pl.ds((t - wide_items) * cols, cols)]

    def own_view(t):
        if t < wide_items:
            return (w_gate, w_up)[t // 4].at[0, pl.ds(t % 4 * piece, piece)]
        return w_down.at[0, :, pl.ds((t - wide_items) * cols, cols)]

    def move(kind, t):
        source, slot, device = (
            (own_view(t), 0, across),
            (view(0, t), 1, partner),
            (view(0, t), 2, sibling),
            (view(1, t), 3, sibling),
        )[kind]
        return pltpu.make_async_remote_copy(
            src_ref=source,
            dst_ref=view(slot, t),
            send_sem=ring_sem.at[0, kind, t],
            recv_sem=ring_sem.at[1, kind, t],
            device_id=device,
            device_id_type=MESH,
        )

    def first_on(t):
        move(1, t).start()
        move(2, t).start()

    def second_on(t):
        move(1, t).wait_recv()
        move(3, t).start()

    def pump(home_items, cross_items, guest_items):
        @pl.when(home)
        def _():
            for t in home_items:
                first_on(t)

        @pl.when(jnp.logical_not(home))
        def _():
            for t in cross_items:
                move(0, t).start()
            for t in guest_items:
                move(0, t).wait_recv()
                first_on(t)

    @pl.when(home)
    def _():
        for load in own_loads:
            load.wait()

    pump(range(0, 1), range(0, 2), ())

    def naming(expert_of):
        named = jnp.zeros((experts, rows), jnp.float32)
        for k in range(TOP):
            named = jnp.where(expert_of == routes_t[k : k + 1, :], 1.0, named)
        return named

    device_of = iota((experts, rows), 0)
    named = naming(device_of // 2 * 2 + side)
    before = (iota((rows, rows), 0) < iota((rows, rows), 1)).astype(jnp.float32)
    rank = dot(named.astype(jnp.bfloat16), before.astype(jnp.bfloat16))
    code_t[...] = jnp.where(named > 0, rank, -1.0).astype(jnp.int32)
    slot = (lax.rem(q, 2) * 2 + iota((experts, share, rows), 0) % 2) * share + iota(
        (experts, share, rows), 1
    )
    pick = (code_t[...][:, None, :] == slot).astype(jnp.float32).reshape(experts * share, rows)
    pick_t[...] = pick.astype(jnp.bfloat16)

    loads[2].wait()
    attn[0 : prefill.shape[0], :] = prefill[...]
    for copy in pack_copies:
        copy.wait()
    packs = pack_all[...]
    sums = packs[:, 0:requests]
    peaks = packs[:, requests : 2 * requests]
    masses = packs[:, 2 * requests : 3 * requests]
    factors = jnp.exp(peaks - jnp.max(peaks, axis=0)[None])
    attn[prefill.shape[0] :, :] = (
        jnp.sum(sums * factors, axis=0) / jnp.sum(masses * factors, axis=0)
    ).astype(jnp.bfloat16)
    state = residual[...].astype(jnp.float32) + dot(attn[...], wobuf[...])
    hidden[...] = state
    scaled = (state * norm_gain[...]).astype(jnp.bfloat16)
    scaled_all[q] = scaled
    squares = jnp.sum(state * state, axis=1, keepdims=True)
    scores_of = lax.dot_general(
        scaled, router_t[...], (((1,), (1,)), ((), ())), preferred_element_type=jnp.float32
    )
    stat = jnp.concatenate([scores_of, jnp.broadcast_to(squares, (rows, 128 - experts))], axis=1)
    stat_all[q] = stat.T[0 : stat_all.shape[1], :]
    stat_copies = exchange(stat_all, stat_sem)
    scaled_copies = exchange(scaled_all, scaled_sem)
    pump(range(1, 3), range(2, 3), range(0, 1))
    def all_to_all(source, target, sems):
        def send(i, carry):
            other = lax.rem(me + i, n_ep)
            pltpu.make_async_remote_copy(
                src_ref=source.at[other],
                dst_ref=target.at[me],
                send_sem=sems.at[0],
                recv_sem=sems.at[1],
                device_id={"ep": other},
                device_id_type=MESH,
            ).start()
            return carry

        lax.fori_loop(1, n_ep, send, 0)
        own = pltpu.make_async_copy(source.at[me], target.at[me], sems.at[2])
        own.start()

        def received():
            own.wait()
            rest = target.at[pl.ds(0, n_ep - 1)]
            pltpu.make_async_copy(rest, rest, sems.at[1]).wait()

        def sent():
            rest = source.at[pl.ds(0, n_ep - 1)]
            pltpu.make_async_copy(rest, rest, sems.at[0]).wait()

        return received, sent

    order = (0, 3, 1, 2)
    out_waits = []

    def dispatch(i):
        picked = dot(pick_t[...], scaled_all[lax.rem(q + order[i], n_kv)])
        sends[i] = picked.reshape(experts, share, cols).astype(jnp.bfloat16)
        out_waits.append(all_to_all(sends.at[i], arrived.at[i], out_sem.at[i]))

    dispatch(0)
    for copy in stat_copies:
        copy.wait()
    stats = stat_all[0]
    for j in range(1, n_kv):
        stats = stats + stat_all[j]
    inv_t = lax.rsqrt(stats[experts : experts + 1, :] / width + epsilon)
    for copy in scaled_copies:
        copy.wait()
    pump(range(3, 6), range(3, items), range(1, 3))
    dispatch(1)
    pump(range(6, 9), (), range(3, 4))
    dispatch(2)
    pump(range(9, items), (), range(4, 6))
    on_lane = iota((experts, share, rows), 2) == iota((experts, share, rows), 1)
    slot_pick = pick_t[...].astype(jnp.float32).reshape(experts, share, rows)
    slot_inv = jnp.sum(slot_pick * inv_t[None], axis=2, keepdims=True)
    inv_out[...] = jnp.sum(jnp.where(on_lane, slot_inv, 0.0), axis=1, keepdims=True)
    inv_received, inv_sent = all_to_all(inv_out, inv_in, inv_sem)
    dispatch(n_kv - 1)
    pump((), (), range(6, wide_items))
    for t in range(4):
        second_on(t)
    pump((), (), range(wide_items, wide_items + 2))
    for t in range(4, wide_items):
        second_on(t)
    pump((), (), range(wide_items + 2, items))
    logits_t = stats[0:experts, :] * inv_t
    totals = jnp.sum(jnp.where(naming(device_of) > 0, jnp.exp(logits_t), 0.0), axis=0, keepdims=True)
    turned = jnp.where(side == 0, pltpu.roll(logits_t, 1, 0), pltpu.roll(logits_t, experts - 1, 0))
    served = jnp.where(device_of % 2 == side, logits_t, turned)
    gate_t = jnp.where(code_t[...] >= 0, jnp.exp(served), 0.0) / totals
    mix_high, mix_low = split_two(
        (
            jnp.broadcast_to(gate_t[:, None, :], (experts, share, rows))
            .reshape(experts * share, rows)
            * pick_t[...].astype(jnp.float32)
        ).T
    )
    tile_blocks = 32
    tile_rows = tile_blocks * share

    hidden_cols = gates.shape[2]

    def expert_in(c, first, last):
        def tile(m, carry):
            block = pl.multiple_of(m * tile_blocks, tile_blocks)
            row = pl.multiple_of(m * tile_rows, tile_rows)
            if first == 0:
                g = jnp.zeros((tile_rows, hidden_cols), jnp.float32)
                u = jnp.zeros((tile_rows, hidden_cols), jnp.float32)
            else:
                g = total[c, 0, pl.ds(row, tile_rows), :]
                u = total[c, 1, pl.ds(row, tile_rows), :]
            for i in range(first, last):
                off = order[i]
                x = arrived[i, pl.ds(block, tile_blocks)].reshape(tile_rows, cols)
                some = pl.ds(pl.multiple_of(lax.rem(q + off, n_kv) * cols, cols), cols)
                g = g + dot(x, gates[c, some, :])
                u = u + dot(x, ups[c, some, :])
            if last < n_kv:
                total[c, 0, pl.ds(row, tile_rows), :] = g
                total[c, 1, pl.ds(row, tile_rows), :] = u
            else:
                g = g * inv_wide[pl.ds(row, tile_rows), :]
                u = u * inv_wide[pl.ds(row, tile_rows), :]
                act = (g / (1.0 + jnp.exp(-g)) * u).astype(jnp.bfloat16)
                acts[c, pl.ds(row, tile_rows), :] = act
            return carry

        lax.fori_loop(0, n_ep // tile_blocks, tile, 0)

    def expert_out(n):
        span = pl.ds(n * cols, cols)

        def tile(m, carry):
            block = pl.multiple_of(m * tile_blocks, tile_blocks)
            row = pl.multiple_of(m * tile_rows, tile_rows)
            term = jnp.zeros((tile_rows, cols), jnp.float32)
            for c in range(n_kv):
                term = term + dot(acts[c, pl.ds(row, tile_rows), :], downs[c, :, span])
            replies[n, pl.ds(block, tile_blocks)] = term.reshape(
                tile_blocks, share, cols
            ).astype(jnp.bfloat16)
            return carry

        lax.fori_loop(0, n_ep // tile_blocks, tile, 0)

    for i in range(n_kv - 1):
        out_waits[i][0]()
    for c in range(n_kv):
        if c >= 2:
            for t in range(wide_items):
                move(c, t).wait_recv()
        expert_in(c, 0, n_kv - 1)
    inv_received()
    slot_inv = jnp.sum(
        jnp.where(on_lane, jnp.broadcast_to(inv_in[...], (experts, share, rows)), 0.0),
        axis=2,
        keepdims=True,
    ).reshape(experts * share, 1)
    inv_wide[...] = jnp.broadcast_to(slot_inv, inv_wide.shape)
    out_waits[n_kv - 1][0]()
    for c in range(n_kv):
        expert_in(c, n_kv - 1, n_kv)
    second_on(wide_items)
    back_waits = []
    for n in range(n_kv):
        if n + 1 < n_kv:
            second_on(wide_items + n + 1)
        for kind in range(2, 4):
            move(kind, wide_items + n).wait_recv()
        expert_out(n)
        back_waits.append(all_to_all(replies.at[n], returned.at[n], back_sem.at[n]))
    for _, sent in out_waits:
        sent()
    inv_sent()
    for t in range(items):
        for kind in range(1, 4):
            move(kind, t).wait_send()

    @pl.when(jnp.logical_not(home))
    def _():
        for t in range(items):
            move(0, t).wait_send()

    def part_copy(n):
        place = lax.rem(q - n + n_kv, n_kv) - 1
        return pltpu.make_async_remote_copy(
            src_ref=part_out.at[n],
            dst_ref=part_in.at[place],
            send_sem=part_sem.at[0, n],
            recv_sem=part_sem.at[1, place],
            device_id={"kv": n},
            device_id_type=MESH,
        )

    for n in range(n_kv):
        back_waits[n][0]()
        back = returned[n].reshape(experts * share, cols)
        part_out[n] = (dot(mix_high, back) + dot(mix_low, back)).astype(jnp.bfloat16)

        @pl.when(q != n)
        def _():
            part_copy(n).start()

    combined = hidden[...] + part_out[q].astype(jnp.float32)
    for d in range(1, n_kv):
        pltpu.make_async_copy(part_in.at[d - 1], part_in.at[d - 1], part_sem.at[1, d - 1]).wait()
        combined = combined + part_in[d - 1].astype(jnp.float32)
    own_square = jnp.sum(combined * combined, axis=1, keepdims=True)
    square_all[q] = jnp.broadcast_to(own_square, (rows, 128)).T[0:8, :]
    square_copies = exchange(square_all, square_sem)
    for _, sent in back_waits:
        sent()
    for n in range(n_kv):

        @pl.when(q != n)
        def _():
            part_copy(n).wait_send()

    for copy in square_copies:
        copy.wait()
    square = square_all[0]
    for j in range(1, n_kv):
        square = square + square_all[j]
    inv_row = lax.rsqrt(square[0:1] / width + epsilon)
    inv_second = jnp.broadcast_to(inv_row, (128, rows)).T[:, 0:1]
    out[...] = (combined * inv_second * final_gain[...]).astype(out.dtype)


def make_per_device(n_ep, n_kv):
    def per_device(
        queries,
        key_pool,
        value_pool,
        page_table,
        lengths,
        prefill_attn,
        residual,
        w_out,
        norm_gain,
        router,
        w_gate,
        w_up,
        w_down,
        final_gain,
        routes,
    ):
        width = queries.shape[1]
        rows, cols = residual.shape
        experts = router.shape[1]
        share = min(rows, 2 * rows * TOP // experts) // n_kv
        tokens = key_pool.shape[0] * key_pool.shape[1]
        packed = 3 * queries.shape[0]
        f32, bf16 = jnp.float32, jnp.bfloat16
        vmem = pl.BlockSpec(memory_space=pltpu.VMEM)
        smem = pl.BlockSpec(memory_space=pltpu.SMEM)
        anywhere = pl.BlockSpec(memory_space=pl.ANY)
        dma = pltpu.SemaphoreType.DMA
        return pl.pallas_call(
            lambda *refs: layer_kernel(n_ep, n_kv, *refs),
            name="layer",
            out_shape=jax.ShapeDtypeStruct((rows, cols), bf16),
            in_specs=[vmem, anywhere, anywhere, smem, smem, vmem, vmem, anywhere, vmem, vmem]
            + [anywhere] * 3
            + [vmem, vmem],
            out_specs=vmem,
            scratch_shapes=[
                pltpu.VMEM((tokens, width), bf16),
                pltpu.VMEM((tokens, width), bf16),
                pltpu.VMEM(w_out.shape, bf16),
                pltpu.VMEM((rows, width), bf16),
                pltpu.VMEM((n_kv, packed, width), f32),
                pltpu.VMEM((n_kv, experts + 8, rows), f32),
                pltpu.VMEM((n_kv, rows, cols), bf16),
                pltpu.VMEM((rows, cols), f32),
                pltpu.VMEM((experts, rows), jnp.int32),
                pltpu.VMEM((experts * share, rows), bf16),
                pltpu.VMEM((n_kv, experts, share, cols), bf16),
                pltpu.VMEM((n_kv, experts, share, cols), bf16),
                pltpu.VMEM((n_kv,) + w_gate.shape[1:], bf16),
                pltpu.VMEM((n_kv,) + w_up.shape[1:], bf16),
                pltpu.VMEM((n_kv,) + w_down.shape[1:], bf16),
                pltpu.VMEM((experts, 1, rows), f32),
                pltpu.VMEM((experts, 1, rows), f32),
                pltpu.VMEM((experts * share, w_gate.shape[2]), f32),
                pltpu.VMEM((n_kv, 2, experts * share, w_gate.shape[2]), f32),
                pltpu.VMEM((n_kv, experts * share, w_gate.shape[2]), bf16),
                pltpu.VMEM((n_kv, experts, share, cols), bf16),
                pltpu.VMEM((n_kv, experts, share, cols), bf16),
                pltpu.VMEM((n_kv, rows, cols), bf16),
                pltpu.VMEM((n_kv - 1, rows, cols), bf16),
                pltpu.VMEM((n_kv, 8, rows), f32),
                dma((6,)),
                dma((2, n_kv - 1)),
                dma((2, n_kv - 1)),
                dma((2, n_kv - 1)),
                dma((2, 4, 12)),
                dma((3,)),
                dma((n_kv, 3)),
                dma((n_kv, 3)),
                dma((2, n_kv)),
                dma((2, n_kv - 1)),
            ],
            compiler_params=pltpu.CompilerParams(
                collective_id=0, has_side_effects=True, vmem_limit_bytes=60 << 20
            ),
        )(
            queries,
            key_pool.reshape(tokens, width),
            value_pool.reshape(tokens, width),
            page_table,
            lengths,
            prefill_attn,
            residual,
            w_out,
            norm_gain.reshape(1, cols),
            router.T,
            w_gate,
            w_up,
            w_down,
            final_gain.reshape(1, cols),
            routes.T,
        )

    return per_device


def solution(mesh):
    placed = (
        P("ep", None),
        P(("ep", "kv"), None, None),
        P(("ep", "kv"), None, None),
        P("ep", "kv", None),
        P("ep"),
        P("ep", None),
        P("ep", "kv"),
        P(None, "kv"),
        P("kv"),
        P("kv", None),
        P("ep", None, "kv"),
        P("ep", None, "kv"),
        P("ep", "kv", None),
        P("kv"),
        P("ep", None),
    )
    return jax.shard_map(
        make_per_device(mesh.shape["ep"], mesh.shape["kv"]),
        mesh=mesh,
        in_specs=placed,
        out_specs=P("ep", "kv"),
        check_vma=False,
    )
```
